1024 devices in a mesh: exp: 64 (over y, x, core), attn: 16 (over z).
Axes of the slice: x: 4, y: 8, z: 16, core: 2. Of those that a mesh axis runs over, the one named last changes fastest.
Arguments:
- tokens: bfloat16 [8192, 2048], P('exp', 'attn'), may hold values from -6 to 6
- cotangent: bfloat16 [8192, 2048], P('exp', 'attn'), may hold values from -6 to 6
- expert_ids: int32 [8192, 2], P('exp'), may hold values from 0 to 63, all different within a row; in each aligned block of 128 rows (0 to 127, 128 to 255, ...) at most 6 rows name the same one
- route_weight: bfloat16 [8192, 2], P('exp'), may hold values from 0.099609375 to 1
- gate_weight: bfloat16 [64, 2048, 768], P('exp', 'attn'), may hold values from -0.125 to 0.125
- up_weight: bfloat16 [64, 2048, 768], P('exp', 'attn'), may hold values from -0.125 to 0.125
- down_weight: bfloat16 [64, 768, 2048], P('exp', None, 'attn'), may hold values from -0.21875 to 0.21875
Outputs:
- grad_tokens: bfloat16 [8192, 2048], P('exp', 'attn')
- grad_route: float32 [8192, 2], P('exp')
- grad_gate: float32 [64, 2048, 768], P('exp', 'attn')
- grad_up: float32 [64, 2048, 768], P('exp', 'attn')
- grad_down: float32 [64, 768, 2048], P('exp', None, 'attn')
The draws below stay inside these ranges and needn't reach their ends.
Inputs may be any that keep to these rules, and one draw needn't show every extreme that they name: `expert_ids`: each row names 2 different experts. Within the 128 tokens of one index of exp (aligned blocks of rows), no expert is named by more than 6 choices, and in every draw some block names some expert exactly 6 times.
All inputs are finite; a program needn't handle non-finite values.
Results may differ from the reference program's by a relative error of at most 0.028.
Values may be sent and summed in bfloat16 or wider, within the bound.
No kernel may reach another device: no remote copies, remote signals or barrier semaphores. Data moves between devices by JAX's collectives and lax.ppermute only.
A program may use at most 32 MiB of HBM per device.

```python
import math
import jax
import jax.numpy as jnp
import numpy as np
from jax import lax

D = 2048
H = 768
TOK_DEV = 128
TOPW = 2
EXPERTS = 64
CAP = 6
ROWS = 384
TOKENS = 8192
N_EXP = 64
N_ATTN = 16


def shard_levels(key, shape, split, least, largest):
    gain, own = 1.0, jax.random.fold_in(key, 6)
    for position, shards_of in split:
        steps = jnp.exp(jax.random.uniform(jax.random.fold_in(own, position), (shards_of,), jnp.float32, least / len(split), largest / len(split)))
        gain = gain * jnp.repeat(steps, shape[position] // shards_of).reshape([-1 if axis == position else 1 for axis in range(len(shape))])
    return gain


def deal_out(own_key, own, number, rows, amount, top, most, slope):
    sequence = jax.random.permutation(own_key, amount)
    packed, common = load_shares(amount, rows * top, most, slope, True), load_shares(amount, rows * top, most, slope, False)
    places = jnp.arange(amount)

    def named(sizes, rotation):
        used = int((sizes > 0).sum())
        fixed = max(1, used // 4)
        passed = fixed + (places - fixed + rotation * (used - fixed)) % max(1, amount - fixed)
        return jnp.zeros((amount,), jnp.int32).at[sequence[jnp.where(places < fixed, places, passed)]].set(jnp.asarray(sizes, jnp.int32))

    sizes = jnp.where(number % 4 == 0, named(packed, number // 4), named(common, number - number // 4 - 1))
    mixed = jax.random.permutation(jax.random.fold_in(own, 3), amount)
    giver, receiver = mixed[0:amount // 2 * 2:2], mixed[1:amount // 2 * 2:2]
    room = jnp.minimum(sizes[giver] - 1, most - sizes[receiver]) // 2
    room = jnp.where((giver == sequence[0]) | (receiver == sequence[0]) | (sizes[receiver] == 0), 0, jnp.maximum(room, 0))
    passed = jax.random.randint(jax.random.fold_in(own, 4), (amount // 2,), 0, 1 << 20) % (room + 1)
    sizes = sizes.at[giver].add(-passed).at[receiver].add(passed)
    labels = jnp.searchsorted(jnp.cumsum(sizes), jnp.arange(rows * top), side="right").astype(jnp.int32)
    grid = labels.reshape(top, rows).T
    grid = grid[jax.random.permutation(jax.random.fold_in(own, 1), rows)]
    rotation = jax.random.randint(jax.random.fold_in(own, 2), (rows, 1), 0, top)
    return jnp.take_along_axis(grid, (jnp.arange(top)[None, :] + rotation) % top, axis=1)


def load_shares(amount, total, most, skew, full):
    portions = [(1 << 20) // math.isqrt(grade ** skew) + 1 for grade in range(1, amount + 1)]
    largest = most if full else min(most, max(-(-total // amount), total * portions[0] // sum(portions)))
    least = 1 if total - largest >= amount - 1 else 0
    counts, surplus = [largest] + [least] * (amount - 1), total - largest - least * (amount - 1)
    while surplus > 0:
        free = [i for i in range(1, amount) if counts[i] < largest] or [i for i in range(1, amount) if counts[i] < most]
        mass, budget = sum([portions[i] for i in free]), surplus
        for i in free:
            extra = min(most - counts[i], max(1, budget * portions[i] // mass), surplus)
            counts[i] = counts[i] + extra
            surplus = surplus - extra
    return np.array(counts)


def noise(key, dims, scale, most, shards=(), kind=jnp.bfloat16):
    level = shard_levels(key, dims, shards, -0.22, 0.18) if shards else 1.0
    values = jax.random.normal(key, dims, jnp.float32) * scale * level
    return jnp.minimum(jnp.maximum(values, -most), most).astype(kind)


def setup_inputs(seed: int = 0) -> dict:
    key_of = jax.random.split(jax.random.key(seed), 8)
    tokens = noise(key_of[0], (TOKENS, D), 1.0, 6.0, ((0, 64), (1, 16)))
    cotangent = noise(key_of[1], (TOKENS, D), 1.0, 6.0, ((0, 64), (1, 16)))
    expert_ids_keys = jax.random.split(jax.random.fold_in(key_of[2], 1), TOKENS // TOK_DEV)
    expert_ids_turns = jax.random.permutation(jax.random.fold_in(key_of[2], 3), TOKENS // TOK_DEV)
    expert_ids = jax.vmap(lambda own, number: deal_out(jax.random.fold_in(key_of[2], 2), own, number, TOK_DEV, EXPERTS, TOPW, CAP, 2))(expert_ids_keys, expert_ids_turns).reshape((TOKENS, TOPW))
    route_weight = jnp.clip(jnp.exp(math.log(1.0) - 2.306499 * jax.random.uniform(key_of[3], (TOKENS, TOPW), jnp.float32) ** shard_levels(key_of[3], (TOKENS, TOPW), ((0, 64),), -0.2, 0.2)), 0.099609375, 1.0).astype(jnp.bfloat16)
    gate_weight = noise(key_of[4], (EXPERTS, D, H), D ** -0.5, 0.125, ((0, 64), (1, 16)))
    up_weight = noise(key_of[5], (EXPERTS, D, H), D ** -0.5, 0.125, ((0, 64), (1, 16)))
    down_weight = noise(key_of[6], (EXPERTS, H, D), H ** -0.5, 0.21875, ((0, 64), (2, 16)))
    return dict(tokens=tokens, cotangent=cotangent, expert_ids=expert_ids, route_weight=route_weight, gate_weight=gate_weight, up_weight=up_weight, down_weight=down_weight)


def slice_sums(left_side, right_side):
    row_total = left_side.shape[0]
    partials = jnp.einsum('rnd,ndh->nrh', left_side.reshape(row_total, N_ATTN, -1).astype(jnp.float32), right_side.reshape(N_ATTN, -1, right_side.shape[1]).astype(jnp.float32))
    rounded = lax.optimization_barrier(partials.astype(jnp.bfloat16))
    return jnp.sum(rounded.astype(jnp.float32), axis=0)


def reference(tokens, cotangent, expert_ids, route_weight, gate_weight, up_weight, down_weight):
    per_block = TOK_DEV * TOPW
    routed = expert_ids.reshape(N_EXP, per_block)
    one_hot = (routed[:, :, None] == jnp.arange(EXPERTS, dtype=jnp.int32)[None, None, :]).astype(jnp.int32)
    ranked = jnp.cumsum(one_hot, axis=1) - 1
    slot_pos = jnp.sum(ranked * one_hot, axis=2)
    sources = jnp.arange(N_EXP, dtype=jnp.int32)[:, None]
    column = (sources * CAP + slot_pos).astype(jnp.int32)
    row_index = (sources * per_block + jnp.arange(per_block, dtype=jnp.int32)[None, :]).astype(jnp.int32)
    slot_table = jnp.full((EXPERTS, ROWS), N_EXP * per_block, jnp.int32).at[routed, column].set(row_index)
    feat_all = jnp.concatenate([jnp.repeat(tokens, TOPW, axis=0), jnp.zeros((1, D), jnp.bfloat16)], axis=0)
    upstream_all = jnp.concatenate([jnp.repeat(cotangent, TOPW, axis=0), jnp.zeros((1, D), jnp.bfloat16)], axis=0)
    weight_all = jnp.concatenate([route_weight.reshape(-1), jnp.zeros((1,), jnp.bfloat16)], axis=0)

    def one_expert(inputs):
        table_row, gate_w, up_w, down_w = inputs
        feat_rows = feat_all[table_row]
        upstream_rows = upstream_all[table_row]
        weight_rows = weight_all[table_row]
        scaled_rows = (weight_rows[:, None].astype(jnp.float32) * upstream_rows.astype(jnp.float32)).astype(jnp.bfloat16)
        gate_sum = slice_sums(feat_rows, gate_w)
        up_sum = slice_sums(feat_rows, up_w)
        back_sum = slice_sums(scaled_rows, down_w.T)
        sigmoid_gate = jax.nn.sigmoid(gate_sum)
        silu_gate = gate_sum * sigmoid_gate
        activation = (silu_gate * up_sum).astype(jnp.bfloat16)
        grad_g = (back_sum * up_sum * sigmoid_gate * (1.0 + gate_sum * (1.0 - sigmoid_gate))).astype(jnp.bfloat16)
        grad_u = (back_sum * silu_gate).astype(jnp.bfloat16)
        grad_gate_e = jnp.dot(feat_rows.T, grad_g, preferred_element_type=jnp.float32)
        grad_up_e = jnp.dot(feat_rows.T, grad_u, preferred_element_type=jnp.float32)
        grad_down_e = jnp.dot(activation.T, scaled_rows, preferred_element_type=jnp.float32)
        term_rows = (jnp.dot(grad_g, gate_w.T, preferred_element_type=jnp.float32) + jnp.dot(grad_u, up_w.T, preferred_element_type=jnp.float32)).astype(jnp.bfloat16)
        out_rows = jnp.dot(activation, down_w, preferred_element_type=jnp.float32)
        score_parts = jnp.sum((upstream_rows.astype(jnp.float32) * out_rows).reshape(ROWS, N_ATTN, -1), axis=2)
        score_rounded = lax.optimization_barrier(score_parts.astype(jnp.bfloat16))
        score_rows = jnp.sum(score_rounded.astype(jnp.float32), axis=1)
        return grad_gate_e, grad_up_e, grad_down_e, term_rows, score_rows

    grad_gate, grad_up, grad_down, term_all, score_all = lax.map(one_expert, (slot_table, gate_weight, up_weight, down_weight))
    flat_table = slot_table.reshape(-1)
    token_sums = jnp.zeros((N_EXP * per_block + 1, D), jnp.float32).at[flat_table].add(term_all.reshape(-1, D).astype(jnp.float32))
    grad_tokens = jnp.sum(token_sums[:-1].reshape(TOKENS, TOPW, D), axis=1).astype(jnp.bfloat16)
    score_sums = jnp.zeros((N_EXP * per_block + 1,), jnp.float32).at[flat_table].add(score_all.reshape(-1))
    grad_route = score_sums[:-1].reshape(TOKENS, TOPW)
    return grad_tokens, grad_route, grad_gate, grad_up, grad_down
```

```python
import functools

import jax
import jax.numpy as jnp
from jax import lax
from jax.experimental import pallas as pl
from jax.experimental.pallas import tpu as pltpu
from jax.sharding import PartitionSpec as P

F32 = jnp.float32
BF16 = jnp.bfloat16
PAD = 8


def iota(shape, axis):
    return lax.broadcasted_iota(jnp.int32, shape, axis)


def one_hot(mask):
    return jnp.where(mask, 1.0, 0.0).astype(BF16)


def mm(a, b, ca, cb):
    return lax.dot_general(a, b, (((ca,), (cb,)), ((), ())), preferred_element_type=F32)


def pack_kernel(ids_ref, weight_ref, tok_ref, cot_ref, send_ref, rank_ref):
    top, tok = ids_ref.shape
    rows = send_ref.shape[0]
    width = tok_ref.shape[1]
    ids = ids_ref[...]
    weight = weight_ref[...].astype(F32)
    row, col = iota((tok, tok), 0), iota((tok, tok), 1)
    columns = [
        jnp.sum(jnp.where(row == col, ids[j : j + 1, :], 0), axis=1, keepdims=True)
        for j in range(top)
    ]
    ranks, hots, scaled = [], [], []
    slot = iota((rows, tok), 0)
    for j in range(top):
        same = [jnp.where((columns[i] == ids[j : j + 1, :]) & (row < col), 1, 0) for i in range(top)]
        rank = jnp.sum(functools.reduce(jnp.add, same), axis=0, keepdims=True)
        ranks.append(rank)
        hit = slot == ids[j : j + 1, :] * PAD + rank
        hots.append(jnp.where(hit, 1.0, 0.0))
        scaled.append(jnp.where(hit, weight[j : j + 1, :], 0.0))
    rank_ref[...] = jnp.concatenate(ranks, axis=0)
    plain = functools.reduce(jnp.add, hots).astype(BF16)
    heavy = functools.reduce(jnp.add, scaled).astype(BF16)
    send_ref[:, :width] = mm(plain, tok_ref[...], 1, 0).astype(BF16)
    send_ref[:, width:] = mm(heavy, cot_ref[...], 1, 0).astype(BF16)


def partial_kernel(cap, recv_ref, gate_ref, up_ref, down_ref, rows_ref, part_ref):
    step = pl.program_id(0)
    slots, padded = rows_ref.shape[0], recv_ref.shape[0]
    width = gate_ref.shape[0]

    @pl.when(step == 0)
    def _():
        s, r = iota((slots, padded), 0), iota((slots, padded), 1)
        keep = one_hot(((r >> 3) * cap + (r & 7) == s) & ((r & 7) < cap))
        rows_ref[...] = mm(keep, recv_ref[...], 1, 0).astype(BF16)
        part_ref[...] = mm(rows_ref[:, :width], gate_ref[...], 1, 0).astype(BF16)

    @pl.when(step == 1)
    def _():
        part_ref[...] = mm(rows_ref[:, :width], up_ref[...], 1, 0).astype(BF16)

    @pl.when(step == 2)
    def _():
        part_ref[...] = mm(rows_ref[:, width:], down_ref[...], 1, 1).astype(BF16)


def sum_kernel(parts, part_ref, out_ref):
    n = part_ref.shape[0] // parts
    total = part_ref[0:n, :].astype(F32)
    for i in range(1, parts):
        total = total + part_ref[i * n : (i + 1) * n, :].astype(F32)
    total = total.astype(BF16)
    for i in range(parts):
        out_ref[i * n : (i + 1) * n, :] = total


def grad_kernel(
    cap,
    rows_ref,
    gate_sum_ref,
    up_sum_ref,
    back_sum_ref,
    gate_ref,
    up_ref,
    down_ref,
    grad_gate_ref,
    grad_up_ref,
    grad_down_ref,
    send_ref,
    term_ref,
    score_ref,
):
    step = pl.program_id(0)
    slots = rows_ref.shape[0]
    width = gate_ref.shape[0]
    gate = gate_sum_ref[...].astype(F32)
    up = up_sum_ref[...].astype(F32)
    back = back_sum_ref[...].astype(F32)
    sig = jax.nn.sigmoid(gate)
    silu = gate * sig
    act_wide = silu * up
    act = act_wide.astype(BF16)
    grad_g = (back * up * sig * (1.0 + gate * (1.0 - sig))).astype(BF16)
    grad_u = (back * silu).astype(BF16)
    feat, scaled = rows_ref[:, :width], rows_ref[:, width:]
    grad_gate_ref[...] = mm(feat, grad_g, 0, 0)
    grad_up_ref[...] = mm(feat, grad_u, 0, 0)
    grad_down_ref[...] = mm(act, scaled, 0, 0)
    term = mm(grad_g, gate_ref[...], 1, 1) + mm(grad_u, up_ref[...], 1, 1)
    score = jnp.sum(act.astype(F32) * back, axis=1, keepdims=True)

    @pl.when(step == 0)
    def _():
        term_ref[...] = term
        score_ref[...] = jnp.broadcast_to(score, score_ref.shape)

    @pl.when(step > 0)
    def _():
        term_ref[...] += term
        score_ref[...] += jnp.broadcast_to(score, score_ref.shape)

    @pl.when(step == pl.num_programs(0) - 1)
    def _():
        padded = send_ref.shape[0]
        r, s = iota((padded, slots), 0), iota((padded, slots), 1)
        spread = one_hot(((r >> 3) * cap + (r & 7) == s) & ((r & 7) < cap))
        base = (r >> 3) * cap
        block = one_hot(((r & 7) == cap) & (s >= base) & (s < base + cap))
        s2, lane = iota((slots, width), 0), iota((slots, width), 1)
        own = jnp.where(lax.rem(s2, cap) == lane, score_ref[...], 0.0).astype(BF16)
        send_ref[...] = (
            mm(spread, term_ref[...].astype(BF16), 1, 0) + mm(block, own, 1, 0)
        ).astype(BF16)


def merge_kernel(cap, ids_ref, rank_ref, weight_ref, recv_ref, tok_ref, route_ref):
    top, tok = ids_ref.shape
    rows, width = recv_ref.shape
    recv = recv_ref[...]
    slot = iota((rows, tok), 0)
    sub = iota((width, tok), 0)
    hots, scores = [], []
    for j in range(top):
        ids, rank = ids_ref[j : j + 1, :], rank_ref[j : j + 1, :]
        hots.append(jnp.where(slot == ids * PAD + rank, 1.0, 0.0))
        line = mm(recv, one_hot(slot == ids * PAD + cap), 0, 0)
        scores.append(jnp.sum(jnp.where(sub == rank, line, 0.0), axis=0, keepdims=True))
    tok_ref[...] = mm(functools.reduce(jnp.add, hots).astype(BF16), recv, 0, 0).astype(BF16)
    route_ref[...] = jnp.concatenate(scores, axis=0) / weight_ref[...].astype(F32)


def full(shape):
    return pl.BlockSpec(shape, lambda k: (0,) * len(shape))


def exchange(rows, axis):
    n = lax.axis_size(axis)
    blocks = rows.reshape(n, rows.shape[0] // n, rows.shape[1])
    blocks = lax.all_to_all(blocks, axis, split_axis=0, concat_axis=0, tiled=True)
    return blocks.reshape(rows.shape)


def shards(tokens, cotangent, expert_ids, route_weight, gate_weight, up_weight, down_weight):
    tok, width = tokens.shape
    top = expert_ids.shape[1]
    experts, parts = lax.axis_size("exp"), lax.axis_size("attn")
    cap = 3 * tok * top // (2 * experts)
    hidden = gate_weight.shape[2]
    slots, padded = experts * cap, experts * PAD
    ids, weight = expert_ids.T, route_weight.T
    gate_w, up_w, down_w = gate_weight[0], up_weight[0], down_weight[0]

    send, rank = pl.pallas_call(
        pack_kernel,
        out_shape=(
            jax.ShapeDtypeStruct((padded, 2 * width), BF16),
            jax.ShapeDtypeStruct((top, tok), jnp.int32),
        ),
        name="pack",
    )(ids, weight, tokens, cotangent)
    recv = exchange(send, "exp")
    rows, part = pl.pallas_call(
        functools.partial(partial_kernel, cap),
        grid=(3,),
        out_shape=(
            jax.ShapeDtypeStruct((slots, 2 * width), BF16),
            jax.ShapeDtypeStruct((slots, 3 * hidden), BF16),
        ),
        in_specs=[
            full((padded, 2 * width)),
            full((width, hidden)),
            full((width, hidden)),
            full((hidden, width)),
        ],
        out_specs=(
            full((slots, 2 * width)),
            pl.BlockSpec((slots, hidden), lambda k: (0, k)),
        ),
        name="partial",
    )(recv, gate_w, up_w, down_w)
    summed = pl.pallas_call(
        functools.partial(sum_kernel, parts),
        out_shape=jax.ShapeDtypeStruct((slots, 3 * hidden), BF16),
        name="sums",
    )(exchange(part, "attn"))
    summed = exchange(summed, "attn")
    n = 3
    piece = hidden // n
    grad_gate, grad_up, grad_down, back = pl.pallas_call(
        functools.partial(grad_kernel, cap),
        grid=(n,),
        out_shape=(
            jax.ShapeDtypeStruct((width, hidden), F32),
            jax.ShapeDtypeStruct((width, hidden), F32),
            jax.ShapeDtypeStruct((hidden, width), F32),
            jax.ShapeDtypeStruct((padded, width), BF16),
        ),
        in_specs=[
            full((slots, 2 * width)),
            pl.BlockSpec((slots, piece), lambda k: (0, k)),
            pl.BlockSpec((slots, piece), lambda k: (0, n + k)),
            pl.BlockSpec((slots, piece), lambda k: (0, 2 * n + k)),
            pl.BlockSpec((width, piece), lambda k: (0, k)),
            pl.BlockSpec((width, piece), lambda k: (0, k)),
            pl.BlockSpec((piece, width), lambda k: (k, 0)),
        ],
        out_specs=(
            pl.BlockSpec((width, piece), lambda k: (0, k)),
            pl.BlockSpec((width, piece), lambda k: (0, k)),
            pl.BlockSpec((piece, width), lambda k: (k, 0)),
            full((padded, width)),
        ),
        scratch_shapes=[pltpu.VMEM((slots, width), F32), pltpu.VMEM((slots, width), F32)],
        name="grads",
    )(rows, summed, summed, summed, gate_w, up_w, down_w)
    grad_tokens, grad_route = pl.pallas_call(
        functools.partial(merge_kernel, cap),
        out_shape=(
            jax.ShapeDtypeStruct((tok, width), BF16),
            jax.ShapeDtypeStruct((top, tok), F32),
        ),
        name="merge",
    )(ids, rank, weight, exchange(back, "exp"))
    return grad_tokens, grad_route.T, grad_gate[None], grad_up[None], grad_down[None]


def solution(mesh):
    in_specs = (
        P("exp", "attn"),
        P("exp", "attn"),
        P("exp", None),
        P("exp", None),
        P("exp", "attn", None),
        P("exp", "attn", None),
        P("exp", None, "attn"),
    )
    out_specs = (
        P("exp", "attn"),
        P("exp", None),
        P("exp", "attn", None),
        P("exp", "attn", None),
        P("exp", None, "attn"),
    )
    return jax.shard_map(shards, mesh=mesh, in_specs=in_specs, out_specs=out_specs, check_vma=False)
```

```python
import functools
import math

import jax
import jax.numpy as jnp
from jax import lax
from jax.experimental import pallas as pl
from jax.sharding import PartitionSpec as P

F32 = jnp.float32
BF16 = jnp.bfloat16
PAD = 8


def iota(shape, axis):
    return lax.broadcasted_iota(jnp.int32, shape, axis)


def one_hot(mask):
    return jnp.where(mask, 1.0, 0.0).astype(BF16)


def mm(a, b, ca, cb):
    return lax.dot_general(a, b, (((ca,), (cb,)), ((), ())), preferred_element_type=F32)


def pack_kernel(ids_ref, weight_ref, tok_ref, cot_ref, send_ref, rank_ref):
    top, tok = ids_ref.shape
    rows = send_ref.shape[0]
    width = tok_ref.shape[1]
    ids = ids_ref[...]
    weight = weight_ref[...].astype(F32)
    row, col = iota((tok, tok), 0), iota((tok, tok), 1)
    columns = [
        jnp.sum(jnp.where(row == col, ids[j : j + 1, :], 0), axis=1, keepdims=True)
        for j in range(top)
    ]
    ranks, hots, scaled = [], [], []
    slot = iota((rows, tok), 0)
    for j in range(top):
        same = [jnp.where((columns[i] == ids[j : j + 1, :]) & (row < col), 1, 0) for i in range(top)]
        rank = jnp.sum(functools.reduce(jnp.add, same), axis=0, keepdims=True)
        ranks.append(rank)
        hit = slot == ids[j : j + 1, :] * PAD + rank
        hots.append(jnp.where(hit, 1.0, 0.0))
        scaled.append(jnp.where(hit, weight[j : j + 1, :], 0.0))
    rank_ref[...] = jnp.concatenate(ranks, axis=0)
    plain = functools.reduce(jnp.add, hots).astype(BF16)
    heavy = functools.reduce(jnp.add, scaled).astype(BF16)
    send_ref[:, :width] = mm(plain, tok_ref[...], 1, 0).astype(BF16)
    send_ref[:, width:] = mm(heavy, cot_ref[...], 1, 0).astype(BF16)


def spread_kernel(cap, local, recv_ref, gate_ref, up_ref, down_ref, out_ref):
    padded = recv_ref.shape[0]
    width, hidden = gate_ref.shape
    slots = padded // PAD * cap
    piece = hidden // local
    block = out_ref.shape[0] // local
    s, r = iota((slots, padded), 0), iota((slots, padded), 1)
    keep = one_hot(((r >> 3) * cap + (r & 7) == s) & ((r & 7) < cap))
    rows = mm(keep, recv_ref[...], 1, 0).astype(BF16)
    eye = one_hot(iota((width, width), 0) == iota((width, width), 1))
    turned = [mm(ref[...], eye, 0, 0).astype(BF16) for ref in (gate_ref, up_ref)]
    for p in range(local):
        at = p * block
        out_ref[at : at + slots, :] = rows[:, :width]
        out_ref[at + slots : at + 2 * slots, :] = rows[:, width:]
        at += 2 * slots
        for m in range(2):
            out_ref[at : at + piece, :] = turned[m][p * piece : (p + 1) * piece, :]
            at += piece
        out_ref[at : at + piece, :] = down_ref[p * piece : (p + 1) * piece, :]


def partial_kernel(slots, local, strided, held_ref, part_ref):
    block = held_ref.shape[0] // local
    piece = (block - 2 * slots) // 3
    chunk = piece // strided
    for m in range(3):
        total = None
        for f in range(local):
            at = f * block
            rows = held_ref[at : at + slots, :] if m < 2 else held_ref[at + slots : at + 2 * slots, :]
            at += 2 * slots + m * piece
            term = mm(held_ref[at : at + piece, :], rows, 1, 1)
            total = term if total is None else total + term
        total = total.astype(BF16)
        for q in range(strided):
            to = (q * 3 + m) * chunk
            part_ref[to : to + chunk, :] = total[q * chunk : (q + 1) * chunk, :]


def act_kernel(strided, part_ref, out_ref):
    n = part_ref.shape[0] // strided
    chunk = n // 3
    total = part_ref[0:n, :].astype(F32)
    for q in range(1, strided):
        total = total + part_ref[q * n : (q + 1) * n, :].astype(F32)
    gate, up, back = (total[m * chunk : (m + 1) * chunk, :] for m in range(3))
    sig = jax.nn.sigmoid(gate)
    silu = gate * sig
    act = (silu * up).astype(BF16)
    grad_g = (back * up * sig * (1.0 + gate * (1.0 - sig))).astype(BF16)
    grad_u = (back * silu).astype(BF16)
    score = jnp.sum(act.astype(F32) * back, axis=0, keepdims=True)
    score = jnp.where(iota((PAD, score.shape[1]), 0) == 0, score, 0.0).astype(BF16)
    m = out_ref.shape[0] // strided
    for q in range(strided):
        at = q * m
        out_ref[at : at + chunk, :] = act
        out_ref[at + chunk : at + 2 * chunk, :] = grad_g
        out_ref[at + 2 * chunk : at + n, :] = grad_u
        out_ref[at + n : at + m, :] = score


def grad_kernel(local, strided, held_ref, acts_ref, out_ref):
    slots = acts_ref.shape[1]
    width = held_ref.shape[1]
    block = held_ref.shape[0] // local
    piece = (block - 2 * slots) // 3
    m = acts_ref.shape[0] // strided
    chunk = (m - PAD) // 3
    act, grad_g, grad_u = (
        jnp.concatenate(
            [acts_ref[q * m + k * chunk : q * m + (k + 1) * chunk, :] for q in range(strided)], axis=0
        )
        for k in range(3)
    )
    score = acts_ref[3 * chunk : 3 * chunk + PAD, :].astype(F32)
    for q in range(1, strided):
        score = score + acts_ref[q * m + 3 * chunk : (q + 1) * m, :].astype(F32)
    lines = slots // width
    score = jnp.concatenate(
        [score[0:1, k * width : (k + 1) * width] for k in range(lines)]
        + [jnp.zeros((PAD - lines, width), F32)],
        axis=0,
    ).astype(BF16)
    out = out_ref.shape[0] // local
    for f in range(local):
        at = f * block
        feat, scaled = held_ref[at : at + slots, :], held_ref[at + slots : at + 2 * slots, :]
        at += 2 * slots
        gate_w, up_w = held_ref[at : at + piece, :], held_ref[at + piece : at + 2 * piece, :]
        to = f * out
        out_ref[to : to + slots, :] = (mm(grad_g, gate_w, 0, 0) + mm(grad_u, up_w, 0, 0)).astype(BF16)
        out_ref[to + slots : to + slots + PAD, :] = score
        to += slots + PAD
        out_ref[to : to + piece, :] = mm(grad_g, feat, 1, 0).astype(BF16)
        out_ref[to + piece : to + 2 * piece, :] = mm(grad_u, feat, 1, 0).astype(BF16)
        out_ref[to + 2 * piece : to + 3 * piece, :] = mm(act, scaled, 1, 0).astype(BF16)


def back_kernel(cap, slots, local, got_ref, send_ref):
    padded, width = send_ref.shape
    block = got_ref.shape[0] // local
    term = got_ref[0 : slots + PAD, :].astype(F32)
    for f in range(1, local):
        term = term + got_ref[f * block : f * block + slots + PAD, :].astype(F32)
    lines = slots // width
    score = jnp.concatenate([term[slots + k : slots + k + 1, :] for k in range(lines)], axis=1)
    term = term[:slots, :].astype(BF16)
    r, s = iota((padded, slots), 0), iota((padded, slots), 1)
    spread = one_hot(((r >> 3) * cap + (r & 7) == s) & ((r & 7) < cap))
    base = (r >> 3) * cap
    mine = ((r & 7) == cap) & (s >= base) & (s < base + cap)
    scores = jnp.where(mine, score, 0.0).astype(BF16)
    lane = one_hot(lax.rem(iota((slots, width), 0), cap) == iota((slots, width), 1))
    send_ref[...] = (mm(spread, term, 1, 0) + mm(scores, lane, 1, 0)).astype(BF16)


def out_kernel(skip, local, got_ref, grad_gate_ref, grad_up_ref, grad_down_ref):
    block = got_ref.shape[0] // local
    width = got_ref.shape[1]
    piece = (block - skip) // 3
    eye = one_hot(iota((width, width), 0) == iota((width, width), 1))
    gate, up, down = (
        jnp.concatenate(
            [got_ref[f * block + skip + m * piece : f * block + skip + (m + 1) * piece, :] for f in range(local)],
            axis=0,
        )
        for m in range(3)
    )
    grad_gate_ref[...] = mm(eye, gate, 1, 1)
    grad_up_ref[...] = mm(eye, up, 1, 1)
    grad_down_ref[...] = down.astype(F32)


def merge_kernel(cap, ids_ref, rank_ref, weight_ref, recv_ref, tok_ref, route_ref):
    top, tok = ids_ref.shape
    rows, width = recv_ref.shape
    recv = recv_ref[...]
    slot = iota((rows, tok), 0)
    sub = iota((width, tok), 0)
    hots, scores = [], []
    for j in range(top):
        ids, rank = ids_ref[j : j + 1, :], rank_ref[j : j + 1, :]
        hots.append(jnp.where(slot == ids * PAD + rank, 1.0, 0.0))
        line = mm(recv, one_hot(slot == ids * PAD + cap), 0, 0)
        scores.append(jnp.sum(jnp.where(sub == rank, line, 0.0), axis=0, keepdims=True))
    tok_ref[...] = mm(functools.reduce(jnp.add, hots).astype(BF16), recv, 0, 0).astype(BF16)
    route_ref[...] = jnp.concatenate(scores, axis=0) / weight_ref[...].astype(F32)


def exchange(rows, axis, groups=None):
    n = lax.axis_size(axis) if groups is None else len(groups[0])
    blocks = rows.reshape(n, rows.shape[0] // n, rows.shape[1])
    blocks = lax.all_to_all(
        blocks, axis, split_axis=0, concat_axis=0, tiled=True, axis_index_groups=groups
    )
    return blocks.reshape(rows.shape)


def shape_of(*dims, dtype=BF16):
    return jax.ShapeDtypeStruct(dims, dtype)


def shards(tokens, cotangent, expert_ids, route_weight, gate_weight, up_weight, down_weight):
    tok, width = tokens.shape
    top = expert_ids.shape[1]
    experts, parts = lax.axis_size("exp"), lax.axis_size("attn")
    cap = 3 * tok * top // (2 * experts)
    hidden = gate_weight.shape[2]
    slots, padded = experts * cap, experts * PAD
    local = math.isqrt(parts)
    strided = parts // local
    piece = hidden // local
    near = [[q * local + r for r in range(local)] for q in range(strided)]
    far = [[q * local + r for q in range(strided)] for r in range(local)]
    ids, weight = expert_ids.T, route_weight.T
    gate_w, up_w, down_w = gate_weight[0], up_weight[0], down_weight[0]

    send, rank = pl.pallas_call(
        pack_kernel,
        out_shape=(shape_of(padded, 2 * width), shape_of(top, tok, dtype=jnp.int32)),
        name="pack",
    )(ids, weight, tokens, cotangent)
    recv = exchange(send, "exp")
    held = pl.pallas_call(
        functools.partial(spread_kernel, cap, local),
        out_shape=shape_of(local * (2 * slots + 3 * piece), width),
        name="spread",
    )(recv, gate_w, up_w, down_w)
    held = exchange(held, "attn", near)
    part = pl.pallas_call(
        functools.partial(partial_kernel, slots, local, strided),
        out_shape=shape_of(3 * piece, slots),
        name="partial",
    )(held)
    part = exchange(part, "attn", far)
    acts = pl.pallas_call(
        functools.partial(act_kernel, strided),
        out_shape=shape_of(3 * piece + strided * PAD, slots),
        name="acts",
    )(part)
    acts = exchange(acts, "attn", far)
    got = pl.pallas_call(
        functools.partial(grad_kernel, local, strided),
        out_shape=shape_of(local * (slots + PAD + 3 * piece), width),
        name="grads",
    )(held, acts)
    got = exchange(got, "attn", near)
    back = pl.pallas_call(
        functools.partial(back_kernel, cap, slots, local),
        out_shape=shape_of(padded, width),
        name="back",
    )(got)
    back = exchange(back, "exp")
    grad_gate, grad_up, grad_down = pl.pallas_call(
        functools.partial(out_kernel, slots + PAD, local),
        out_shape=(
            shape_of(width, hidden, dtype=F32),
            shape_of(width, hidden, dtype=F32),
            shape_of(hidden, width, dtype=F32),
        ),
        name="out",
    )(got)
    grad_tokens, grad_route = pl.pallas_call(
        functools.partial(merge_kernel, cap),
        out_shape=(shape_of(tok, width), shape_of(top, tok, dtype=F32)),
        name="merge",
    )(ids, rank, weight, back)
    return grad_tokens, grad_route.T, grad_gate[None], grad_up[None], grad_down[None]


def solution(mesh):
    in_specs = (
        P("exp", "attn"),
        P("exp", "attn"),
        P("exp", None),
        P("exp", None),
        P("exp", "attn", None),
        P("exp", "attn", None),
        P("exp", None, "attn"),
    )
    out_specs = (
        P("exp", "attn"),
        P("exp", None),
        P("exp", "attn", None),
        P("exp", "attn", None),
        P("exp", None, "attn"),
    )
    return jax.shard_map(shards, mesh=mesh, in_specs=in_specs, out_specs=out_specs, check_vma=False)
```

```python
import functools
import math

import jax
import jax.numpy as jnp
from jax import lax
from jax.experimental import pallas as pl
from jax.experimental.pallas import tpu as pltpu
from jax.sharding import PartitionSpec as P

F32 = jnp.float32
BF16 = jnp.bfloat16
VMEM = 67043328
PAD = 8


def iota(shape, axis):
    return lax.broadcasted_iota(jnp.int32, shape, axis)


def one_hot(mask):
    return jnp.where(mask, 1.0, 0.0).astype(BF16)


def mm(a, b, ca, cb):
    return lax.dot_general(a, b, (((ca,), (cb,)), ((), ())), preferred_element_type=F32)


def pack_kernel(ready, ids_ref, weight_ref, tok_ref, cot_ref, send_ref, rank_ref):
    ready()
    top, tok = ids_ref.shape
    rows = send_ref.shape[0]
    width = tok_ref.shape[1]
    ids = ids_ref[...]
    weight = weight_ref[...].astype(F32)
    row, col = iota((tok, tok), 0), iota((tok, tok), 1)
    columns = [
        jnp.sum(jnp.where(row == col, ids[j : j + 1, :], 0), axis=1, keepdims=True)
        for j in range(top)
    ]
    ranks, hots, scaled = [], [], []
    slot = iota((rows, tok), 0)
    for j in range(top):
        same = [jnp.where((columns[i] == ids[j : j + 1, :]) & (row < col), 1, 0) for i in range(top)]
        rank = jnp.sum(functools.reduce(jnp.add, same), axis=0, keepdims=True)
        ranks.append(rank)
        hit = slot == ids[j : j + 1, :] * PAD + rank
        hots.append(jnp.where(hit, 1.0, 0.0))
        scaled.append(jnp.where(hit, weight[j : j + 1, :], 0.0))
    rank_ref[...] = jnp.concatenate(ranks, axis=0)
    plain = functools.reduce(jnp.add, hots).astype(BF16)
    heavy = functools.reduce(jnp.add, scaled).astype(BF16)
    send_ref[:, :width] = mm(plain, tok_ref[...], 1, 0).astype(BF16)
    send_ref[:, width:] = mm(heavy, cot_ref[...], 1, 0).astype(BF16)


def spread_kernel(cap, local, ready, recv_ref, gate_ref, up_ref, down_ref, out_ref):
    padded = recv_ref.shape[0]
    width, hidden = gate_ref.shape
    slots = padded // PAD * cap
    piece = hidden // local
    block = out_ref.shape[0] // local
    s, r = iota((slots, padded), 0), iota((slots, padded), 1)
    keep = one_hot(((r >> 3) * cap + (r & 7) == s) & ((r & 7) < cap))
    rows = mm(keep, recv_ref[...], 1, 0).astype(BF16)
    eye = one_hot(iota((width, width), 0) == iota((width, width), 1))
    ready()
    turned = [mm(ref[...], eye, 0, 0).astype(BF16) for ref in (gate_ref, up_ref)]
    for p in range(local):
        at = p * block
        out_ref[at : at + slots, :] = rows[:, :width]
        out_ref[at + slots : at + 2 * slots, :] = rows[:, width:]
        at += 2 * slots
        for m in range(2):
            out_ref[at : at + piece, :] = turned[m][p * piece : (p + 1) * piece, :]
            at += piece
        out_ref[at : at + piece, :] = down_ref[p * piece : (p + 1) * piece, :]


def partial_kernel(slots, local, strided, held_ref, part_ref):
    block = held_ref.shape[0] // local
    piece = (block - 2 * slots) // 3
    chunk = piece // strided
    for m in range(3):
        total = None
        for f in range(local):
            at = f * block
            rows = held_ref[at : at + slots, :] if m < 2 else held_ref[at + slots : at + 2 * slots, :]
            at += 2 * slots + m * piece
            term = mm(held_ref[at : at + piece, :], rows, 1, 1)
            total = term if total is None else total + term
        total = total.astype(BF16)
        for q in range(strided):
            to = (q * 3 + m) * chunk
            part_ref[to : to + chunk, :] = total[q * chunk : (q + 1) * chunk, :]


def act_kernel(strided, part_ref, out_ref):
    n = part_ref.shape[0] // strided
    chunk = n // 3
    total = part_ref[0:n, :].astype(F32)
    for q in range(1, strided):
        total = total + part_ref[q * n : (q + 1) * n, :].astype(F32)
    gate, up, back = (total[m * chunk : (m + 1) * chunk, :] for m in range(3))
    sig = jax.nn.sigmoid(gate)
    silu = gate * sig
    act = (silu * up).astype(BF16)
    grad_g = (back * up * sig * (1.0 + gate * (1.0 - sig))).astype(BF16)
    grad_u = (back * silu).astype(BF16)
    score = jnp.sum(act.astype(F32) * back, axis=0, keepdims=True)
    score = jnp.where(iota((PAD, score.shape[1]), 0) == 0, score, 0.0).astype(BF16)
    m = out_ref.shape[0] // strided
    for q in range(strided):
        at = q * m
        out_ref[at : at + chunk, :] = act
        out_ref[at + chunk : at + 2 * chunk, :] = grad_g
        out_ref[at + 2 * chunk : at + n, :] = grad_u
        out_ref[at + n : at + m, :] = score


def grad_kernel(local, strided, held_ref, acts_ref, out_ref):
    slots = acts_ref.shape[1]
    width = held_ref.shape[1]
    block = held_ref.shape[0] // local
    piece = (block - 2 * slots) // 3
    m = acts_ref.shape[0] // strided
    chunk = (m - PAD) // 3
    act, grad_g, grad_u = (
        jnp.concatenate(
            [acts_ref[q * m + k * chunk : q * m + (k + 1) * chunk, :] for q in range(strided)], axis=0
        )
        for k in range(3)
    )
    score = acts_ref[3 * chunk : 3 * chunk + PAD, :].astype(F32)
    for q in range(1, strided):
        score = score + acts_ref[q * m + 3 * chunk : (q + 1) * m, :].astype(F32)
    lines = slots // width
    score = jnp.concatenate(
        [score[0:1, k * width : (k + 1) * width] for k in range(lines)]
        + [jnp.zeros((PAD - lines, width), F32)],
        axis=0,
    ).astype(BF16)
    out = out_ref.shape[0] // local
    for f in range(local):
        at = f * block
        feat, scaled = held_ref[at : at + slots, :], held_ref[at + slots : at + 2 * slots, :]
        at += 2 * slots
        gate_w, up_w = held_ref[at : at + piece, :], held_ref[at + piece : at + 2 * piece, :]
        to = f * out
        out_ref[to : to + slots, :] = (mm(grad_g, gate_w, 0, 0) + mm(grad_u, up_w, 0, 0)).astype(BF16)
        out_ref[to + slots : to + slots + PAD, :] = score
        to += slots + PAD
        out_ref[to : to + piece, :] = mm(grad_g, feat, 1, 0).astype(BF16)
        out_ref[to + piece : to + 2 * piece, :] = mm(grad_u, feat, 1, 0).astype(BF16)
        out_ref[to + 2 * piece : to + 3 * piece, :] = mm(act, scaled, 1, 0).astype(BF16)


def back_kernel(cap, slots, local, got_ref, send_ref):
    padded, width = send_ref.shape
    block = got_ref.shape[0] // local
    term = got_ref[0 : slots + PAD, :].astype(F32)
    for f in range(1, local):
        term = term + got_ref[f * block : f * block + slots + PAD, :].astype(F32)
    lines = slots // width
    score = jnp.concatenate([term[slots + k : slots + k + 1, :] for k in range(lines)], axis=1)
    term = term[:slots, :].astype(BF16)
    r, s = iota((padded, slots), 0), iota((padded, slots), 1)
    spread = one_hot(((r >> 3) * cap + (r & 7) == s) & ((r & 7) < cap))
    base = (r >> 3) * cap
    mine = ((r & 7) == cap) & (s >= base) & (s < base + cap)
    scores = jnp.where(mine, score, 0.0).astype(BF16)
    lane = one_hot(lax.rem(iota((slots, width), 0), cap) == iota((slots, width), 1))
    send_ref[...] = (mm(spread, term, 1, 0) + mm(scores, lane, 1, 0)).astype(BF16)


def out_kernel(skip, local, got_ref, grad_gate_ref, grad_up_ref, grad_down_ref):
    block = got_ref.shape[0] // local
    width = got_ref.shape[1]
    piece = (block - skip) // 3
    eye = one_hot(iota((width, width), 0) == iota((width, width), 1))
    gate, up, down = (
        jnp.concatenate(
            [got_ref[f * block + skip + m * piece : f * block + skip + (m + 1) * piece, :] for f in range(local)],
            axis=0,
        )
        for m in range(3)
    )
    grad_gate_ref[...] = mm(eye, gate, 1, 1)
    grad_up_ref[...] = mm(eye, up, 1, 1)
    grad_down_ref[...] = down.astype(F32)


def merge_kernel(cap, ids_ref, rank_ref, weight_ref, recv_ref, tok_ref, route_ref):
    top, tok = ids_ref.shape
    rows, width = recv_ref.shape
    recv = recv_ref[...]
    slot = iota((rows, tok), 0)
    sub = iota((width, tok), 0)
    hots, scores = [], []
    for j in range(top):
        ids, rank = ids_ref[j : j + 1, :], rank_ref[j : j + 1, :]
        hots.append(jnp.where(slot == ids * PAD + rank, 1.0, 0.0))
        line = mm(recv, one_hot(slot == ids * PAD + cap), 0, 0)
        scores.append(jnp.sum(jnp.where(sub == rank, line, 0.0), axis=0, keepdims=True))
    tok_ref[...] = mm(functools.reduce(jnp.add, hots).astype(BF16), recv, 0, 0).astype(BF16)
    route_ref[...] = jnp.concatenate(scores, axis=0) / weight_ref[...].astype(F32)


def exchange(rows, axis, groups=None):
    n = lax.axis_size(axis) if groups is None else len(groups[0])
    axis = axis if groups is None else ("exp", "attn")
    blocks = rows.reshape(n, rows.shape[0] // n, rows.shape[1])
    blocks = lax.all_to_all(
        blocks, axis, split_axis=0, concat_axis=0, tiled=True, axis_index_groups=groups
    )
    return blocks.reshape(rows.shape)


def device_groups(experts, parts, local):
    strided, near, far = parts // local, [], []
    for e in range(experts):
        shift = e % 2 * (local // 2)
        place = [
            [
                e * parts + (q * local + (r ^ (local // 2 if 2 * q >= strided else 0)) + shift) % parts
                for r in range(local)
            ]
            for q in range(strided)
        ]
        near += place
        far += [list(column) for column in zip(*place)]
    return near, far


def call(kernel, room=48 * 2**20, **options):
    params = pltpu.CompilerParams(vmem_limit_bytes=VMEM - room)
    return pl.pallas_call(kernel, compiler_params=params, **options)


def call_fetching(kernel, plain, fetched, **options):
    def body(*refs):
        n, m = len(plain), len(fetched)
        sources, held, sem = refs[n : n + m], refs[-1 - m : -1], refs[-1]
        copies = [pltpu.make_async_copy(sources[i], held[i], sem.at[i]) for i in range(m)]
        for copy in copies:
            copy.start()

        def ready():
            for copy in copies:
                copy.wait()

        kernel(ready, *refs[:n], *held, *refs[n + m : -1 - m])

    return call(
        body,
        in_specs=[pl.BlockSpec(memory_space=pltpu.VMEM)] * len(plain)
        + [pl.BlockSpec(memory_space=pltpu.HBM)] * len(fetched),
        scratch_shapes=[pltpu.VMEM(x.shape, x.dtype) for x in fetched]
        + [pltpu.SemaphoreType.DMA((len(fetched),))],
        **options,
    )(*plain, *fetched)


def shape_of(*dims, dtype=BF16):
    return jax.ShapeDtypeStruct(dims, dtype)


def shards(tokens, cotangent, expert_ids, route_weight, gate_weight, up_weight, down_weight):
    tok, width = tokens.shape
    top = expert_ids.shape[1]
    experts, parts = lax.axis_size("exp"), lax.axis_size("attn")
    cap = 3 * tok * top // (2 * experts)
    hidden = gate_weight.shape[2]
    slots, padded = experts * cap, experts * PAD
    local = math.isqrt(parts)
    strided = parts // local
    piece = hidden // local
    near, far = device_groups(experts, parts, local)
    ids, weight = expert_ids.T, route_weight.T
    gate_w, up_w, down_w = gate_weight[0], up_weight[0], down_weight[0]

    send, rank = call_fetching(
        pack_kernel,
        (),
        (ids, weight, tokens, cotangent),
        out_shape=(shape_of(padded, 2 * width), shape_of(top, tok, dtype=jnp.int32)),
        name="pack",
        room=0,
    )
    recv = exchange(send, "exp")
    held = call_fetching(
        functools.partial(spread_kernel, cap, local),
        (recv,),
        (gate_w, up_w, down_w),
        out_shape=shape_of(local * (2 * slots + 3 * piece), width),
        name="spread",
        room=2 * local * (2 * slots + 3 * piece) * width + 2 * padded * 2 * width + 2**16,
    )
    held = exchange(held, "attn", near)
    part = call(
        functools.partial(partial_kernel, slots, local, strided),
        out_shape=shape_of(3 * piece, slots),
        name="partial",
    )(held)
    part = exchange(part, "attn", far)
    acts = call(
        functools.partial(act_kernel, strided),
        out_shape=shape_of(3 * piece + strided * PAD, slots),
        name="acts",
    )(part)
    acts = exchange(acts, "attn", far)
    got = call(
        functools.partial(grad_kernel, local, strided),
        out_shape=shape_of(local * (slots + PAD + 3 * piece), width),
        name="grads",
    )(held, acts)
    got = exchange(got, "attn", near)
    back = call(
        functools.partial(back_kernel, cap, slots, local),
        out_shape=shape_of(padded, width),
        name="back",
    )(got)
    back = exchange(back, "exp")
    grad_gate, grad_up, grad_down = call(
        functools.partial(out_kernel, slots + PAD, local),
        out_shape=(
            shape_of(width, hidden, dtype=F32),
            shape_of(width, hidden, dtype=F32),
            shape_of(hidden, width, dtype=F32),
        ),
        name="out",
    )(got)
    grad_tokens, grad_route = call(
        functools.partial(merge_kernel, cap),
        out_shape=(shape_of(tok, width), shape_of(top, tok, dtype=F32)),
        name="merge",
    )(ids, rank, weight, back)
    return grad_tokens, grad_route.T, grad_gate[None], grad_up[None], grad_down[None]


def solution(mesh):
    in_specs = (
        P("exp", "attn"),
        P("exp", "attn"),
        P("exp", None),
        P("exp", None),
        P("exp", "attn", None),
        P("exp", "attn", None),
        P("exp", None, "attn"),
    )
    out_specs = (
        P("exp", "attn"),
        P("exp", None),
        P("exp", "attn", None),
        P("exp", "attn", None),
        P("exp", None, "attn"),
    )
    return jax.shard_map(shards, mesh=mesh, in_specs=in_specs, out_specs=out_specs, check_vma=False)
```

```python
import functools
import math

import jax
import jax.numpy as jnp
from jax import lax
from jax.experimental import pallas as pl
from jax.experimental.pallas import tpu as pltpu
from jax.sharding import PartitionSpec as P


F32 = jnp.float32
BF16 = jnp.bfloat16
VMEM = 67043328
PAD = 8


def iota(shape, axis):
    return lax.broadcasted_iota(jnp.int32, shape, axis)


def one_hot(mask):
    return jnp.where(mask, 1.0, 0.0).astype(BF16)


def mm(a, b, ca, cb):
    return lax.dot_general(a, b, (((ca,), (cb,)), ((), ())), preferred_element_type=F32)


def pack_kernel(ready, ids_ref, weight_ref, tok_ref, cot_ref, send_ref, rank_ref):
    ready()
    top, tok = ids_ref.shape
    rows = send_ref.shape[0]
    width = tok_ref.shape[1]
    ids = ids_ref[...]
    weight = weight_ref[...].astype(F32)
    row, col = iota((tok, tok), 0), iota((tok, tok), 1)
    columns = [
        jnp.sum(jnp.where(row == col, ids[j : j + 1, :], 0), axis=1, keepdims=True)
        for j in range(top)
    ]
    ranks, hots, scaled = [], [], []
    slot = iota((rows, tok), 0)
    for j in range(top):
        same = [jnp.where((columns[i] == ids[j : j + 1, :]) & (row < col), 1, 0) for i in range(top)]
        rank = jnp.sum(functools.reduce(jnp.add, same), axis=0, keepdims=True)
        ranks.append(rank)
        hit = slot == ids[j : j + 1, :] * PAD + rank
        hots.append(jnp.where(hit, 1.0, 0.0))
        scaled.append(jnp.where(hit, weight[j : j + 1, :], 0.0))
    rank_ref[...] = jnp.concatenate(ranks, axis=0)
    plain = functools.reduce(jnp.add, hots).astype(BF16)
    heavy = functools.reduce(jnp.add, scaled).astype(BF16)
    send_ref[:, :width] = mm(plain, tok_ref[...], 1, 0).astype(BF16)
    send_ref[:, width:] = mm(heavy, cot_ref[...], 1, 0).astype(BF16)


def turn_kernel(local, ready, near_ref, gate_ref, up_ref, down_ref, *chunk_refs):
    *chunk_refs, held_ref = chunk_refs
    width, hidden = gate_ref.shape
    piece = hidden // local
    eye = one_hot(iota((width, width), 0) == iota((width, width), 1))
    ready()
    for m, ref in enumerate((gate_ref, up_ref)):
        held_ref[m * hidden : (m + 1) * hidden, :] = mm(ref[...], eye, 0, 0).astype(BF16)
    held_ref[2 * hidden : 3 * hidden, :] = down_ref[...]
    for k, chunk_ref in enumerate(chunk_refs):
        peer = near_ref[0] ^ k
        for m in range(3):
            at = pl.multiple_of(m * hidden + peer * piece, piece)
            chunk_ref[m * piece : (m + 1) * piece, :] = held_ref[pl.ds(at, piece), :]


def spread_kernel(cap, local, recv_ref, out_ref):
    padded = recv_ref.shape[0]
    width = out_ref.shape[1]
    slots = padded // PAD * cap
    s, r = iota((slots, padded), 0), iota((slots, padded), 1)
    keep = one_hot(((r >> 3) * cap + (r & 7) == s) & ((r & 7) < cap))
    rows = mm(keep, recv_ref[...], 1, 0).astype(BF16)
    for p in range(local):
        at = p * 2 * slots
        out_ref[at : at + slots, :] = rows[:, :width]
        out_ref[at + slots : at + 2 * slots, :] = rows[:, width:]


def rows_of(held_ref, near_ref, k, slots, scaled):
    at = pl.multiple_of((near_ref[0] ^ k) * (2 * slots) + slots * scaled, 16)
    return held_ref[pl.ds(at, slots), :]


def partial_kernel(slots, strided, near_ref, held_ref, *refs):
    *weight_refs, part_ref = refs
    piece = weight_refs[0].shape[0] // 3
    chunk = piece // strided
    for m in range(3):
        total = None
        for k, weight_ref in enumerate(weight_refs):
            rows = rows_of(held_ref, near_ref, k, slots, m // 2)
            term = mm(weight_ref[m * piece : (m + 1) * piece, :], rows, 1, 1)
            total = term if total is None else total + term
        total = total.astype(BF16)
        for q in range(strided):
            to = (q * 3 + m) * chunk
            part_ref[to : to + chunk, :] = total[q * chunk : (q + 1) * chunk, :]


def act_kernel(strided, part_ref, out_ref):
    n = part_ref.shape[0] // strided
    chunk = n // 3
    total = part_ref[0:n, :].astype(F32)
    for q in range(1, strided):
        total = total + part_ref[q * n : (q + 1) * n, :].astype(F32)
    gate, up, back = (total[m * chunk : (m + 1) * chunk, :] for m in range(3))
    sig = jax.nn.sigmoid(gate)
    silu = gate * sig
    act = (silu * up).astype(BF16)
    grad_g = (back * up * sig * (1.0 + gate * (1.0 - sig))).astype(BF16)
    grad_u = (back * silu).astype(BF16)
    score = jnp.sum(act.astype(F32) * back, axis=0, keepdims=True)
    score = jnp.where(iota((PAD, score.shape[1]), 0) == 0, score, 0.0).astype(BF16)
    m = out_ref.shape[0] // strided
    for q in range(strided):
        at = q * m
        out_ref[at : at + chunk, :] = act
        out_ref[at + chunk : at + 2 * chunk, :] = grad_g
        out_ref[at + 2 * chunk : at + n, :] = grad_u
        out_ref[at + n : at + m, :] = score


def acts_of(acts_ref, strided):
    m = acts_ref.shape[0] // strided
    chunk = (m - PAD) // 3
    return [
        jnp.concatenate(
            [acts_ref[q * m + k * chunk : q * m + (k + 1) * chunk, :] for q in range(strided)], axis=0
        )
        for k in range(3)
    ]


def term_kernel(strided, near_ref, acts_ref, *refs):
    *weight_refs, out_ref = refs
    slots = acts_ref.shape[1]
    width = out_ref.shape[1]
    piece = weight_refs[0].shape[0] // 3
    m = acts_ref.shape[0] // strided
    _, grad_g, grad_u = acts_of(acts_ref, strided)
    score = acts_ref[m - PAD : m, :].astype(F32)
    for q in range(1, strided):
        score = score + acts_ref[(q + 1) * m - PAD : (q + 1) * m, :].astype(F32)
    lines = slots // width
    score = jnp.concatenate(
        [score[0:1, k * width : (k + 1) * width] for k in range(lines)]
        + [jnp.zeros((PAD - lines, width), F32)],
        axis=0,
    ).astype(BF16)
    for k, weight_ref in enumerate(weight_refs):
        gate_w, up_w = weight_ref[0:piece, :], weight_ref[piece : 2 * piece, :]
        to = pl.multiple_of((near_ref[0] ^ k) * (slots + PAD), PAD)
        out_ref[pl.ds(to, slots), :] = (mm(grad_g, gate_w, 0, 0) + mm(grad_u, up_w, 0, 0)).astype(BF16)
        out_ref[pl.ds(to + slots, PAD), :] = score


def grad_kernel(strided, near_ref, held_ref, acts_ref, back_ref, *out_refs):
    slots = acts_ref.shape[1]
    piece = out_refs[0].shape[0] // 3
    act, grad_g, grad_u = acts_of(acts_ref, strided)
    for k, out_ref in enumerate(out_refs):
        feat = rows_of(held_ref, near_ref, k, slots, 0)
        scaled = rows_of(held_ref, near_ref, k, slots, 1)
        out_ref[0:piece, :] = mm(grad_g, feat, 1, 0).astype(BF16)
        out_ref[piece : 2 * piece, :] = mm(grad_u, feat, 1, 0).astype(BF16)
        out_ref[2 * piece : 3 * piece, :] = mm(act, scaled, 1, 0).astype(BF16)


def back_kernel(cap, slots, local, got_ref, send_ref):
    padded, width = send_ref.shape
    block = got_ref.shape[0] // local
    term = got_ref[0 : slots + PAD, :].astype(F32)
    for f in range(1, local):
        term = term + got_ref[f * block : f * block + slots + PAD, :].astype(F32)
    lines = slots // width
    score = jnp.concatenate([term[slots + k : slots + k + 1, :] for k in range(lines)], axis=1)
    term = term[:slots, :].astype(BF16)
    r, s = iota((padded, slots), 0), iota((padded, slots), 1)
    spread = one_hot(((r >> 3) * cap + (r & 7) == s) & ((r & 7) < cap))
    base = (r >> 3) * cap
    mine = ((r & 7) == cap) & (s >= base) & (s < base + cap)
    scores = jnp.where(mine, score, 0.0).astype(BF16)
    lane = one_hot(lax.rem(iota((slots, width), 0), cap) == iota((slots, width), 1))
    send_ref[...] = (mm(spread, term, 1, 0) + mm(scores, lane, 1, 0)).astype(BF16)


def out_kernel(near_ref, *refs):
    *got_refs, grad_gate_ref, grad_up_ref, grad_down_ref, held_ref = refs
    piece, width = got_refs[0].shape[0] // 3, got_refs[0].shape[1]
    hidden = piece * len(got_refs)
    for k, got_ref in enumerate(got_refs):
        for m in range(3):
            at = pl.multiple_of(m * hidden + (near_ref[0] ^ k) * piece, piece)
            held_ref[pl.ds(at, piece), :] = got_ref[m * piece : (m + 1) * piece, :]
    eye = one_hot(iota((width, width), 0) == iota((width, width), 1))
    grad_gate_ref[...] = mm(eye, held_ref[0:hidden, :], 1, 1)
    grad_up_ref[...] = mm(eye, held_ref[hidden : 2 * hidden, :], 1, 1)
    grad_down_ref[...] = held_ref[2 * hidden :, :].astype(F32)


def merge_kernel(cap, ids_ref, rank_ref, weight_ref, recv_ref, tok_ref, route_ref):
    top, tok = ids_ref.shape
    rows, width = recv_ref.shape
    recv = recv_ref[...]
    slot = iota((rows, tok), 0)
    sub = iota((width, tok), 0)
    hots, scores = [], []
    for j in range(top):
        ids, rank = ids_ref[j : j + 1, :], rank_ref[j : j + 1, :]
        hots.append(jnp.where(slot == ids * PAD + rank, 1.0, 0.0))
        line = mm(recv, one_hot(slot == ids * PAD + cap), 0, 0)
        scores.append(jnp.sum(jnp.where(sub == rank, line, 0.0), axis=0, keepdims=True))
    tok_ref[...] = mm(functools.reduce(jnp.add, hots).astype(BF16), recv, 0, 0).astype(BF16)
    route_ref[...] = jnp.concatenate(scores, axis=0) / weight_ref[...].astype(F32)


def exchange(rows, axis, groups=None):
    n = lax.axis_size(axis) if groups is None else len(groups[0])
    axis = axis if groups is None else ("exp", "attn")
    blocks = rows.reshape(n, rows.shape[0] // n, rows.shape[1])
    blocks = lax.all_to_all(
        blocks, axis, split_axis=0, concat_axis=0, tiled=True, axis_index_groups=groups
    )
    return blocks.reshape(rows.shape)


def device_groups(experts, parts, local):
    strided, near, far = parts // local, [], []
    for e in range(experts):
        shift = e % 2 * (local // 2)
        place = [
            [
                e * parts + (q * local + (r ^ (local // 2 if 2 * q >= strided else 0)) + shift) % parts
                for r in range(local)
            ]
            for q in range(strided)
        ]
        near += place
        far += [list(column) for column in zip(*place)]
    return near, far


def near_number(parts, local):
    strided = parts // local
    at = (lax.axis_index("attn") + parts - lax.axis_index("exp") % 2 * (local // 2)) % parts
    return at % local ^ jnp.where(2 * (at // local) >= strided, local // 2, 0)


def swap(chunks, near):
    out = [chunks[0]]
    for k in range(1, len(chunks)):
        pairs = [(group[r], group[r ^ k]) for group in near for r in range(len(group))]
        out.append(lax.ppermute(chunks[k], ("exp", "attn"), pairs))
    return out


def call(kernel, operands, room=48 * 2**20, **options):
    params = pltpu.CompilerParams(vmem_limit_bytes=VMEM - room)
    specs = [pl.BlockSpec(memory_space=pltpu.SMEM if x.shape == (1,) else pltpu.VMEM) for x in operands]
    return pl.pallas_call(kernel, in_specs=specs, compiler_params=params, **options)(*operands)


def call_fetching(kernel, plain, fetched, scratch=(), **options):
    def body(*refs):
        n, m = len(plain), len(fetched)
        sources, sem = refs[n : n + m], refs[-1]
        held = refs[len(refs) - 1 - m : -1]
        copies = [pltpu.make_async_copy(sources[i], held[i], sem.at[i]) for i in range(m)]
        for copy in copies:
            copy.start()

        def ready():
            for copy in copies:
                copy.wait()

        kernel(ready, *refs[:n], *held, *refs[n + m : len(refs) - 1 - m])

    space = [pltpu.SMEM if x.shape == (1,) else pltpu.VMEM for x in plain] + [pltpu.HBM] * len(fetched)
    return pl.pallas_call(
        body,
        in_specs=[pl.BlockSpec(memory_space=x) for x in space],
        scratch_shapes=list(scratch)
        + [pltpu.VMEM(x.shape, x.dtype) for x in fetched]
        + [pltpu.SemaphoreType.DMA((len(fetched),))],
        compiler_params=pltpu.CompilerParams(vmem_limit_bytes=VMEM),
        **options,
    )(*plain, *fetched)


def shape_of(*dims, dtype=BF16):
    return jax.ShapeDtypeStruct(dims, dtype)


def shards(tokens, cotangent, expert_ids, route_weight, gate_weight, up_weight, down_weight):
    tok, width = tokens.shape
    top = expert_ids.shape[1]
    experts, parts = lax.axis_size("exp"), lax.axis_size("attn")
    cap = 3 * tok * top // (2 * experts)
    hidden = gate_weight.shape[2]
    slots, padded = experts * cap, experts * PAD
    local = math.isqrt(parts)
    strided = parts // local
    piece = hidden // local
    near, far = device_groups(experts, parts, local)
    me = near_number(parts, local).reshape(1)
    ids, weight = expert_ids.T, route_weight.T
    gate_w, up_w, down_w = gate_weight[0], up_weight[0], down_weight[0]

    send, rank = call_fetching(
        pack_kernel,
        (),
        (ids, weight, tokens, cotangent),
        out_shape=(shape_of(padded, 2 * width), shape_of(top, tok, dtype=jnp.int32)),
        name="pack",
    )
    recv = exchange(send, "exp")
    chunks = call_fetching(
        functools.partial(turn_kernel, local),
        (me,),
        (gate_w, up_w, down_w),
        scratch=[pltpu.VMEM((3 * hidden, width), BF16)],
        out_shape=(shape_of(3 * piece, width),) * local,
        name="turn",
    )
    chunks = swap(chunks, near)
    held = call(
        functools.partial(spread_kernel, cap, local),
        (recv,),
        out_shape=shape_of(local * 2 * slots, width),
        name="spread",
    )
    held = exchange(held, "attn", near)
    part = call(
        functools.partial(partial_kernel, slots, strided),
        (me, held, *chunks),
        out_shape=shape_of(3 * piece, slots),
        name="partial",
    )
    part = exchange(part, "attn", far)
    acts = call(
        functools.partial(act_kernel, strided),
        (part,),
        out_shape=shape_of(3 * piece + strided * PAD, slots),
        name="acts",
    )
    acts = exchange(acts, "attn", far)
    terms = call(
        functools.partial(term_kernel, strided),
        (me, acts, *chunks),
        out_shape=shape_of(local * (slots + PAD), width),
        name="terms",
    )
    back = call(
        functools.partial(back_kernel, cap, slots, local),
        (exchange(terms, "attn", near),),
        out_shape=shape_of(padded, width),
        name="back",
    )
    got = call(
        functools.partial(grad_kernel, strided),
        (me, held, acts, back),
        out_shape=(shape_of(3 * piece, width),) * local,
        name="grads",
    )
    got = swap(got, near)
    grad_gate, grad_up, grad_down = call(
        out_kernel,
        (me, *got),
        out_shape=(
            shape_of(width, hidden, dtype=F32),
            shape_of(width, hidden, dtype=F32),
            shape_of(hidden, width, dtype=F32),
        ),
        scratch_shapes=[pltpu.VMEM((3 * hidden, width), BF16)],
        name="out",
    )
    grad_tokens, grad_route = call(
        functools.partial(merge_kernel, cap),
        (ids, rank, weight, exchange(back, "exp")),
        out_shape=(shape_of(tok, width), shape_of(top, tok, dtype=F32)),
        name="merge",
    )
    return grad_tokens, grad_route.T, grad_gate[None], grad_up[None], grad_down[None]


def solution(mesh):
    in_specs = (
        P("exp", "attn"),
        P("exp", "attn"),
        P("exp", None),
        P("exp", None),
        P("exp", "attn", None),
        P("exp", "attn", None),
        P("exp", None, "attn"),
    )
    out_specs = (
        P("exp", "attn"),
        P("exp", None),
        P("exp", "attn", None),
        P("exp", "attn", None),
        P("exp", None, "attn"),
    )
    return jax.shard_map(shards, mesh=mesh, in_specs=in_specs, out_specs=out_specs, check_vma=False)
```

```python
import functools
import math

import jax
import jax.numpy as jnp
from jax import lax
from jax.experimental import pallas as pl
from jax.experimental.pallas import tpu as pltpu
from jax.sharding import PartitionSpec as P


F32 = jnp.float32
BF16 = jnp.bfloat16
VMEM = 67043328
PAD = 8


def iota(shape, axis):
    return lax.broadcasted_iota(jnp.int32, shape, axis)


def one_hot(mask):
    return jnp.where(mask, 1.0, 0.0).astype(BF16)


def mm(a, b, ca, cb):
    return lax.dot_general(a, b, (((ca,), (cb,)), ((), ())), preferred_element_type=F32)


def pack_kernel(ready, ids_ref, weight_ref, tok_ref, cot_ref, send_ref, table_ref):
    ready()
    top, tok = ids_ref.shape
    rows = send_ref.shape[0]
    width = tok_ref.shape[1]
    ids = ids_ref[...]
    weight = weight_ref[...].astype(F32)
    row, col = iota((tok, tok), 0), iota((tok, tok), 1)
    columns = [
        jnp.sum(jnp.where(row == col, ids[j : j + 1, :], 0), axis=1, keepdims=True)
        for j in range(top)
    ]
    ranks, hots, scaled = [], [], []
    slot = iota((rows, tok), 0)
    for j in range(top):
        same = [jnp.where((columns[i] == ids[j : j + 1, :]) & (row < col), 1, 0) for i in range(top)]
        rank = jnp.sum(functools.reduce(jnp.add, same), axis=0, keepdims=True)
        ranks.append(rank)
        hit = slot == ids[j : j + 1, :] * PAD + rank
        hots.append(jnp.where(hit, 1.0, 0.0))
        scaled.append(jnp.where(hit, weight[j : j + 1, :], 0.0))
    firsts = [ids[j : j + 1, :] * PAD for j in range(top)]
    table = jnp.concatenate(firsts + ranks, axis=0).astype(F32)
    table_ref[...] = jnp.concatenate([table, 1.0 / weight], axis=0)
    plain = functools.reduce(jnp.add, hots).astype(BF16)
    heavy = functools.reduce(jnp.add, scaled).astype(BF16)
    send_ref[:, :width] = mm(plain, tok_ref[...], 1, 0).astype(BF16)
    send_ref[:, width:] = mm(heavy, cot_ref[...], 1, 0).astype(BF16)


def turn_kernel(local, ready, near_ref, gate_ref, up_ref, down_ref, *chunk_refs):
    *chunk_refs, held_ref = chunk_refs
    width, hidden = gate_ref.shape
    piece = hidden // local
    eye = one_hot(iota((width, width), 0) == iota((width, width), 1))
    ready()
    for m, ref in enumerate((gate_ref, up_ref)):
        held_ref[m * hidden : (m + 1) * hidden, :] = mm(ref[...], eye, 0, 0).astype(BF16)
    held_ref[2 * hidden : 3 * hidden, :] = down_ref[...]
    for k, chunk_ref in enumerate(chunk_refs):
        peer = near_ref[0] ^ k
        for m in range(3):
            at = pl.multiple_of(m * hidden + peer * piece, piece)
            chunk_ref[m * piece : (m + 1) * piece, :] = held_ref[pl.ds(at, piece), :]


def spread_kernel(cap, local, recv_ref, out_ref):
    padded = recv_ref.shape[0]
    width = out_ref.shape[1]
    slots = padded // PAD * cap
    s, r = iota((slots, padded), 0), iota((slots, padded), 1)
    keep = one_hot(((r >> 3) * cap + (r & 7) == s) & ((r & 7) < cap))
    rows = mm(keep, recv_ref[...], 1, 0).astype(BF16)
    for p in range(local):
        at = p * 2 * slots
        out_ref[at : at + slots, :] = rows[:, :width]
        out_ref[at + slots : at + 2 * slots, :] = rows[:, width:]


def rows_of(held_ref, near_ref, k, slots, scaled):
    at = pl.multiple_of((near_ref[0] ^ k) * (2 * slots) + slots * scaled, 16)
    return held_ref[pl.ds(at, slots), :]


def partial_kernel(slots, strided, near_ref, held_ref, *refs):
    *weight_refs, part_ref = refs
    piece = weight_refs[0].shape[0] // 3
    chunk = piece // strided
    for m in range(3):
        total = None
        for k, weight_ref in enumerate(weight_refs):
            rows = rows_of(held_ref, near_ref, k, slots, m // 2)
            term = mm(weight_ref[m * piece : (m + 1) * piece, :], rows, 1, 1)
            total = term if total is None else total + term
        total = total.astype(BF16)
        for q in range(strided):
            to = (q * 3 + m) * chunk
            part_ref[to : to + chunk, :] = total[q * chunk : (q + 1) * chunk, :]


def act_kernel(strided, part_ref, out_ref):
    n = part_ref.shape[0] // strided
    chunk = n // 3
    total = part_ref[0:n, :].astype(F32)
    for q in range(1, strided):
        total = total + part_ref[q * n : (q + 1) * n, :].astype(F32)
    gate, up, back = (total[m * chunk : (m + 1) * chunk, :] for m in range(3))
    sig = jax.nn.sigmoid(gate)
    silu = gate * sig
    act = (silu * up).astype(BF16)
    grad_g = (back * up * sig * (1.0 + gate * (1.0 - sig))).astype(BF16)
    grad_u = (back * silu).astype(BF16)
    score = jnp.sum(act.astype(F32) * back, axis=0, keepdims=True)
    score = jnp.where(iota((PAD, score.shape[1]), 0) == 0, score, 0.0).astype(BF16)
    m = out_ref.shape[0] // strided
    for q in range(strided):
        at = q * m
        out_ref[at : at + chunk, :] = act
        out_ref[at + chunk : at + 2 * chunk, :] = grad_g
        out_ref[at + 2 * chunk : at + n, :] = grad_u
        out_ref[at + n : at + m, :] = score


def acts_of(acts_ref, strided):
    m = acts_ref.shape[0] // strided
    chunk = (m - PAD) // 3
    return [
        jnp.concatenate(
            [acts_ref[q * m + k * chunk : q * m + (k + 1) * chunk, :] for q in range(strided)], axis=0
        )
        for k in range(3)
    ]


def term_kernel(strided, near_ref, acts_ref, *refs):
    *weight_refs, out_ref = refs
    slots = acts_ref.shape[1]
    width = out_ref.shape[1]
    piece = weight_refs[0].shape[0] // 3
    m = acts_ref.shape[0] // strided
    _, grad_g, grad_u = acts_of(acts_ref, strided)
    score = acts_ref[m - PAD : m, :].astype(F32)
    for q in range(1, strided):
        score = score + acts_ref[(q + 1) * m - PAD : (q + 1) * m, :].astype(F32)
    lines = slots // width
    score = jnp.concatenate(
        [score[0:1, k * width : (k + 1) * width] for k in range(lines)]
        + [jnp.zeros((PAD - lines, width), F32)],
        axis=0,
    ).astype(BF16)
    for k, weight_ref in enumerate(weight_refs):
        gate_w, up_w = weight_ref[0:piece, :], weight_ref[piece : 2 * piece, :]
        to = pl.multiple_of((near_ref[0] ^ k) * (slots + PAD), PAD)
        out_ref[pl.ds(to, slots), :] = (mm(grad_g, gate_w, 0, 0) + mm(grad_u, up_w, 0, 0)).astype(BF16)
        out_ref[pl.ds(to + slots, PAD), :] = score


def grad_kernel(strided, near_ref, held_ref, acts_ref, *out_refs):
    slots = acts_ref.shape[1]
    piece = out_refs[0].shape[0] // 3
    act, grad_g, grad_u = acts_of(acts_ref, strided)
    for k, out_ref in enumerate(out_refs):
        feat = rows_of(held_ref, near_ref, k, slots, 0)
        scaled = rows_of(held_ref, near_ref, k, slots, 1)
        out_ref[0:piece, :] = mm(grad_g, feat, 1, 0).astype(BF16)
        out_ref[piece : 2 * piece, :] = mm(grad_u, feat, 1, 0).astype(BF16)
        out_ref[2 * piece : 3 * piece, :] = mm(act, scaled, 1, 0).astype(BF16)


def back_kernel(cap, slots, local, got_ref, send_ref):
    padded, width = send_ref.shape
    block = got_ref.shape[0] // local
    term = got_ref[0 : slots + PAD, :].astype(F32)
    for f in range(1, local):
        term = term + got_ref[f * block : f * block + slots + PAD, :].astype(F32)
    lines = slots // width
    score = jnp.concatenate([term[slots + k : slots + k + 1, :] for k in range(lines)], axis=1)
    term = term[:slots, :].astype(BF16)
    r, s = iota((padded, slots), 0), iota((padded, slots), 1)
    spread = one_hot(((r >> 3) * cap + (r & 7) == s) & ((r & 7) < cap))
    base = (r >> 3) * cap
    mine = ((r & 7) == cap) & (s >= base) & (s < base + cap)
    scores = jnp.where(mine, score, 0.0).astype(BF16)
    lane = one_hot(lax.rem(iota((slots, width), 0), cap) == iota((slots, width), 1))
    send_ref[...] = (mm(spread, term, 1, 0) + mm(scores, lane, 1, 0)).astype(BF16)


def out_kernel(near_ref, *refs):
    *got_refs, grad_gate_ref, grad_up_ref, grad_down_ref, held_ref = refs
    piece, width = got_refs[0].shape[0] // 3, got_refs[0].shape[1]
    hidden = piece * len(got_refs)
    for k, got_ref in enumerate(got_refs):
        for m in range(3):
            at = pl.multiple_of(m * hidden + (near_ref[0] ^ k) * piece, piece)
            held_ref[pl.ds(at, piece), :] = got_ref[m * piece : (m + 1) * piece, :]
    eye = one_hot(iota((width, width), 0) == iota((width, width), 1))
    grad_gate_ref[...] = mm(eye, held_ref[0:hidden, :], 1, 1)
    grad_up_ref[...] = mm(eye, held_ref[hidden : 2 * hidden, :], 1, 1)
    grad_down_ref[...] = held_ref[2 * hidden :, :].astype(F32)


def merge_kernel(cap, table_ref, recv_ref, tok_ref, route_ref):
    top, tok = route_ref.shape
    rows, width = recv_ref.shape
    recv = recv_ref[...]
    slot = iota((rows, tok), 0)
    sub = iota((width, tok), 0)
    first, rank = (table_ref[i * top : (i + 1) * top, :].astype(jnp.int32) for i in range(2))
    hots, scores = [], []
    for j in range(top):
        at, own = first[j : j + 1, :], rank[j : j + 1, :]
        hots.append(jnp.where(slot == at + own, 1.0, 0.0))
        line = mm(recv, one_hot(slot == at + cap), 0, 0)
        scores.append(jnp.sum(jnp.where(sub == own, line, 0.0), axis=0, keepdims=True))
    tok_ref[...] = mm(functools.reduce(jnp.add, hots).astype(BF16), recv, 0, 0).astype(BF16)
    route_ref[...] = jnp.concatenate(scores, axis=0) * table_ref[2 * top : 3 * top, :]


def exchange(rows, axis, groups=None):
    n = lax.axis_size(axis) if groups is None else len(groups[0])
    axis = axis if groups is None else ("exp", "attn")
    blocks = rows.reshape(n, rows.shape[0] // n, rows.shape[1])
    blocks = lax.all_to_all(
        blocks, axis, split_axis=0, concat_axis=0, tiled=True, axis_index_groups=groups
    )
    return blocks.reshape(rows.shape)


def device_groups(experts, parts, local):
    strided, near, far = parts // local, [], []
    for e in range(experts):
        shift = e % 2 * (local // 2)
        place = [
            [
                e * parts + (q * local + (r ^ (local // 2 if 2 * q >= strided else 0)) + shift) % parts
                for r in range(local)
            ]
            for q in range(strided)
        ]
        near += place
        far += [list(column) for column in zip(*place)]
    return near, far


def near_number(parts, local):
    strided = parts // local
    at = (lax.axis_index("attn") + parts - lax.axis_index("exp") % 2 * (local // 2)) % parts
    return at % local ^ jnp.where(2 * (at // local) >= strided, local // 2, 0)


def swap(chunks, near):
    out = [chunks[0]]
    for k in range(1, len(chunks)):
        pairs = [(group[r], group[r ^ k]) for group in near for r in range(len(group))]
        out.append(lax.ppermute(chunks[k], ("exp", "attn"), pairs))
    return out


def call(kernel, operands, room=48 * 2**20, **options):
    params = pltpu.CompilerParams(vmem_limit_bytes=VMEM - room)
    specs = [pl.BlockSpec(memory_space=pltpu.SMEM if x.shape == (1,) else pltpu.VMEM) for x in operands]
    return pl.pallas_call(kernel, in_specs=specs, compiler_params=params, **options)(*operands)


def call_fetching(kernel, plain, fetched, scratch=(), **options):
    def body(*refs):
        n, m = len(plain), len(fetched)
        sources, sem = refs[n : n + m], refs[-1]
        held = refs[len(refs) - 1 - m : -1]
        copies = [pltpu.make_async_copy(sources[i], held[i], sem.at[i]) for i in range(m)]
        for copy in copies:
            copy.start()

        def ready():
            for copy in copies:
                copy.wait()

        kernel(ready, *refs[:n], *held, *refs[n + m : len(refs) - 1 - m])

    space = [pltpu.SMEM if x.shape == (1,) else pltpu.VMEM for x in plain] + [pltpu.HBM] * len(fetched)
    return pl.pallas_call(
        body,
        in_specs=[pl.BlockSpec(memory_space=x) for x in space],
        scratch_shapes=list(scratch)
        + [pltpu.VMEM(x.shape, x.dtype) for x in fetched]
        + [pltpu.SemaphoreType.DMA((len(fetched),))],
        compiler_params=pltpu.CompilerParams(vmem_limit_bytes=VMEM),
        **options,
    )(*plain, *fetched)


def shape_of(*dims, dtype=BF16):
    return jax.ShapeDtypeStruct(dims, dtype)


def shards(tokens, cotangent, expert_ids, route_weight, gate_weight, up_weight, down_weight):
    tok, width = tokens.shape
    top = expert_ids.shape[1]
    experts, parts = lax.axis_size("exp"), lax.axis_size("attn")
    cap = 3 * tok * top // (2 * experts)
    hidden = gate_weight.shape[2]
    slots, padded = experts * cap, experts * PAD
    local = math.isqrt(parts)
    strided = parts // local
    piece = hidden // local
    near, far = device_groups(experts, parts, local)
    me = near_number(parts, local).reshape(1)
    ids, weight = expert_ids.T, route_weight.T
    gate_w, up_w, down_w = gate_weight[0], up_weight[0], down_weight[0]

    send, table = call_fetching(
        pack_kernel,
        (),
        (ids, weight, tokens, cotangent),
        out_shape=(shape_of(padded, 2 * width), shape_of(3 * top, tok, dtype=F32)),
        name="pack",
    )
    recv = exchange(send, "exp")
    chunks = call_fetching(
        functools.partial(turn_kernel, local),
        (me,),
        (gate_w, up_w, down_w),
        scratch=[pltpu.VMEM((3 * hidden, width), BF16)],
        out_shape=(shape_of(3 * piece, width),) * local,
        name="turn",
    )
    chunks = swap(chunks, near)
    held = call(
        functools.partial(spread_kernel, cap, local),
        (recv,),
        out_shape=shape_of(local * 2 * slots, width),
        name="spread",
    )
    held = exchange(held, "attn", near)
    part = call(
        functools.partial(partial_kernel, slots, strided),
        (me, held, *chunks),
        out_shape=shape_of(3 * piece, slots),
        name="partial",
    )
    part = exchange(part, "attn", far)
    acts = call(
        functools.partial(act_kernel, strided),
        (part,),
        out_shape=shape_of(3 * piece + strided * PAD, slots),
        name="acts",
    )
    acts = exchange(acts, "attn", far)
    terms = call(
        functools.partial(term_kernel, strided),
        (me, acts, *chunks),
        out_shape=shape_of(local * (slots + PAD), width),
        name="terms",
    )
    terms = exchange(terms, "attn", near)
    got = call(
        functools.partial(grad_kernel, strided),
        (me, held, acts),
        out_shape=(shape_of(3 * piece, width),) * local,
        name="grads",
    )
    got = swap(got, near)
    back = call(
        functools.partial(back_kernel, cap, slots, local),
        (terms,),
        out_shape=shape_of(padded, width),
        name="back",
    )
    grad_gate, grad_up, grad_down = call(
        out_kernel,
        (me, *got),
        out_shape=(
            shape_of(width, hidden, dtype=F32),
            shape_of(width, hidden, dtype=F32),
            shape_of(hidden, width, dtype=F32),
        ),
        scratch_shapes=[pltpu.VMEM((3 * hidden, width), BF16)],
        name="out",
    )
    grad_tokens, grad_route = call(
        functools.partial(merge_kernel, cap),
        (table, exchange(back, "exp")),
        out_shape=(shape_of(tok, width), shape_of(top, tok, dtype=F32)),
        name="merge",
    )
    return grad_tokens, grad_route.T, grad_gate[None], grad_up[None], grad_down[None]


def solution(mesh):
    in_specs = (
        P("exp", "attn"),
        P("exp", "attn"),
        P("exp", None),
        P("exp", None),
        P("exp", "attn", None),
        P("exp", "attn", None),
        P("exp", None, "attn"),
    )
    out_specs = (
        P("exp", "attn"),
        P("exp", None),
        P("exp", "attn", None),
        P("exp", "attn", None),
        P("exp", None, "attn"),
    )
    return jax.shard_map(shards, mesh=mesh, in_specs=in_specs, out_specs=out_specs, check_vma=False)
```

```python
import functools
import math

import jax
import jax.numpy as jnp
from jax import lax
from jax.experimental import pallas as pl
from jax.experimental.pallas import tpu as pltpu
from jax.sharding import PartitionSpec as P


F32 = jnp.float32
BF16 = jnp.bfloat16
VMEM = 67043328
PAD = 8


def iota(shape, axis):
    return lax.broadcasted_iota(jnp.int32, shape, axis)


def one_hot(mask):
    return jnp.where(mask, 1.0, 0.0).astype(BF16)


def mm(a, b, ca, cb):
    return lax.dot_general(a, b, (((ca,), (cb,)), ((), ())), preferred_element_type=F32)


def pack_kernel(ready, ids_ref, weight_ref, tok_ref, cot_ref, send_ref, table_ref):
    ready()
    top, tok = ids_ref.shape
    rows = send_ref.shape[0]
    width = tok_ref.shape[1]
    ids = ids_ref[...]
    weight = weight_ref[...].astype(F32)
    row, col = iota((tok, tok), 0), iota((tok, tok), 1)
    columns = [
        jnp.sum(jnp.where(row == col, ids[j : j + 1, :], 0), axis=1, keepdims=True)
        for j in range(top)
    ]
    ranks, hots, scaled = [], [], []
    slot = iota((rows, tok), 0)
    for j in range(top):
        same = [jnp.where((columns[i] == ids[j : j + 1, :]) & (row < col), 1, 0) for i in range(top)]
        rank = jnp.sum(functools.reduce(jnp.add, same), axis=0, keepdims=True)
        ranks.append(rank)
        hit = slot == ids[j : j + 1, :] * PAD + rank
        hots.append(jnp.where(hit, 1.0, 0.0))
        scaled.append(jnp.where(hit, weight[j : j + 1, :], 0.0))
    firsts = [ids[j : j + 1, :] * PAD for j in range(top)]
    table = jnp.concatenate(firsts + ranks, axis=0).astype(F32)
    table_ref[...] = jnp.concatenate([table, 1.0 / weight], axis=0)
    plain = functools.reduce(jnp.add, hots).astype(BF16)
    heavy = functools.reduce(jnp.add, scaled).astype(BF16)
    send_ref[:, :width] = mm(plain, tok_ref[...], 1, 0).astype(BF16)
    send_ref[:, width:] = mm(heavy, cot_ref[...], 1, 0).astype(BF16)


def turn_kernel(local, ready, near_ref, gate_ref, up_ref, down_ref, *chunk_refs):
    *chunk_refs, held_ref = chunk_refs
    width, hidden = gate_ref.shape
    piece = hidden // local
    eye = one_hot(iota((width, width), 0) == iota((width, width), 1))
    ready()
    for m, ref in enumerate((gate_ref, up_ref)):
        held_ref[m * hidden : (m + 1) * hidden, :] = mm(ref[...], eye, 0, 0).astype(BF16)
    held_ref[2 * hidden : 3 * hidden, :] = down_ref[...]
    for k, chunk_ref in enumerate(chunk_refs):
        peer = (near_ref[0] & 15) ^ k
        for m in range(3):
            at = pl.multiple_of(m * hidden + peer * piece, piece)
            chunk_ref[m * piece : (m + 1) * piece, :] = held_ref[pl.ds(at, piece), :]


def spread_kernel(cap, local, recv_ref, out_ref, scaled_ref):
    padded = recv_ref.shape[0]
    slots, width = scaled_ref.shape
    s, r = iota((slots, padded), 0), iota((slots, padded), 1)
    keep = one_hot(((r >> 3) * cap + (r & 7) == s) & ((r & 7) < cap))
    rows = mm(keep, recv_ref[...], 1, 0).astype(BF16)
    for p in range(local):
        out_ref[p * slots : (p + 1) * slots, :] = rows[:, :width]
    scaled_ref[...] = rows[:, width:]


def rows_of(held_ref, me_ref, k, slots):
    return held_ref[pl.ds(pl.multiple_of(((me_ref[0] & 15) ^ k) * slots, 16), slots), :]


def partial_kernel(slots, strided, me_ref, held_ref, *refs):
    *weight_refs, part_ref = refs
    piece = weight_refs[0].shape[0] // 3
    chunk = piece // strided
    for m in range(2):
        total = None
        for k, weight_ref in enumerate(weight_refs):
            rows = rows_of(held_ref, me_ref, k, slots)
            term = mm(weight_ref[m * piece : (m + 1) * piece, :], rows, 1, 1)
            total = term if total is None else total + term
        total = total.astype(BF16)
        for q in range(strided):
            to = (q * 2 + m) * chunk
            part_ref[to : to + chunk, :] = total[q * chunk : (q + 1) * chunk, :]


def upstream_kernel(n, me_ref, *refs):
    scaled_refs, weight_refs, chunk_refs, held_ref = refs[:n], refs[n : 2 * n], refs[2 * n : -1], refs[-1]
    piece = weight_refs[0].shape[0] // 3
    chunk = chunk_refs[0].shape[0]
    total = None
    for scaled_ref, weight_ref in zip(scaled_refs, weight_refs):
        term = mm(weight_ref[2 * piece :, :], scaled_ref[...], 1, 1)
        total = term if total is None else total + term
    held_ref[...] = total.astype(BF16)
    for k, chunk_ref in enumerate(chunk_refs):
        at = pl.multiple_of(((me_ref[0] >> 4) ^ k) * chunk, 16)
        chunk_ref[...] = held_ref[pl.ds(at, chunk), :]


def act_kernel(strided, part_ref, *refs):
    *back_refs, out_ref, act_ref = refs
    n = part_ref.shape[0] // strided
    chunk = n // 2
    total = part_ref[0:n, :].astype(F32)
    for q in range(1, strided):
        total = total + part_ref[q * n : (q + 1) * n, :].astype(F32)
    gate, up = total[:chunk, :], total[chunk:, :]
    back = functools.reduce(jnp.add, [ref[...].astype(F32) for ref in back_refs])
    sig = jax.nn.sigmoid(gate)
    silu = gate * sig
    act = (silu * up).astype(BF16)
    grad_g = (back * up * sig * (1.0 + gate * (1.0 - sig))).astype(BF16)
    grad_u = (back * silu).astype(BF16)
    score = jnp.sum(act.astype(F32) * back, axis=0, keepdims=True)
    score = jnp.where(iota((PAD, score.shape[1]), 0) == 0, score, 0.0).astype(BF16)
    act_ref[...] = act
    m = out_ref.shape[0] // strided
    for q in range(strided):
        at = q * m
        out_ref[at : at + chunk, :] = grad_g
        out_ref[at + chunk : at + n, :] = grad_u
        out_ref[at + n : at + m, :] = score


def pair_of(pair_ref, strided):
    m = pair_ref.shape[0] // strided
    chunk = (m - PAD) // 2
    return [
        jnp.concatenate(
            [pair_ref[q * m + k * chunk : q * m + (k + 1) * chunk, :] for q in range(strided)], axis=0
        )
        for k in range(2)
    ]


def term_kernel(strided, me_ref, pair_ref, *refs):
    *weight_refs, out_ref = refs
    slots = pair_ref.shape[1]
    width = out_ref.shape[1]
    piece = weight_refs[0].shape[0] // 3
    m = pair_ref.shape[0] // strided
    grad_g, grad_u = pair_of(pair_ref, strided)
    score = pair_ref[m - PAD : m, :].astype(F32)
    for q in range(1, strided):
        score = score + pair_ref[(q + 1) * m - PAD : (q + 1) * m, :].astype(F32)
    lines = slots // width
    score = jnp.concatenate(
        [score[0:1, k * width : (k + 1) * width] for k in range(lines)]
        + [jnp.zeros((PAD - lines, width), F32)],
        axis=0,
    ).astype(BF16)
    for k, weight_ref in enumerate(weight_refs):
        gate_w, up_w = weight_ref[0:piece, :], weight_ref[piece : 2 * piece, :]
        to = pl.multiple_of(((me_ref[0] & 15) ^ k) * (slots + PAD), PAD)
        out_ref[pl.ds(to, slots), :] = (mm(grad_g, gate_w, 0, 0) + mm(grad_u, up_w, 0, 0)).astype(BF16)
        out_ref[pl.ds(to + slots, PAD), :] = score


def grad_kernel(strided, local, me_ref, held_ref, pair_ref, *refs):
    act_refs, scaled_refs = refs[:strided], refs[strided : strided + local]
    out_refs, act_ref = refs[strided + local : -1], refs[-1]
    slots = pair_ref.shape[1]
    piece = out_refs[0].shape[0] // 3
    chunk = piece // strided
    grad_g, grad_u = pair_of(pair_ref, strided)
    for k, ref in enumerate(act_refs):
        act_ref[pl.ds(pl.multiple_of(((me_ref[0] >> 4) ^ k) * chunk, 16), chunk), :] = ref[...]
    for k, out_ref in enumerate(out_refs):
        feat = rows_of(held_ref, me_ref, k, slots)
        out_ref[0:piece, :] = mm(grad_g, feat, 1, 0).astype(BF16)
        out_ref[piece : 2 * piece, :] = mm(grad_u, feat, 1, 0).astype(BF16)
        out_ref[2 * piece : 3 * piece, :] = mm(act_ref[...], scaled_refs[k][...], 1, 0).astype(BF16)


def back_kernel(cap, slots, local, got_ref, send_ref):
    padded, width = send_ref.shape
    block = got_ref.shape[0] // local
    term = got_ref[0 : slots + PAD, :].astype(F32)
    for f in range(1, local):
        term = term + got_ref[f * block : f * block + slots + PAD, :].astype(F32)
    lines = slots // width
    score = jnp.concatenate([term[slots + k : slots + k + 1, :] for k in range(lines)], axis=1)
    term = term[:slots, :].astype(BF16)
    r, s = iota((padded, slots), 0), iota((padded, slots), 1)
    spread = one_hot(((r >> 3) * cap + (r & 7) == s) & ((r & 7) < cap))
    base = (r >> 3) * cap
    mine = ((r & 7) == cap) & (s >= base) & (s < base + cap)
    scores = jnp.where(mine, score, 0.0).astype(BF16)
    lane = one_hot(lax.rem(iota((slots, width), 0), cap) == iota((slots, width), 1))
    send_ref[...] = (mm(spread, term, 1, 0) + mm(scores, lane, 1, 0)).astype(BF16)


def out_kernel(near_ref, *refs):
    *got_refs, grad_gate_ref, grad_up_ref, grad_down_ref, held_ref = refs
    piece, width = got_refs[0].shape[0] // 3, got_refs[0].shape[1]
    hidden = piece * len(got_refs)
    for k, got_ref in enumerate(got_refs):
        for m in range(3):
            at = pl.multiple_of(m * hidden + ((near_ref[0] & 15) ^ k) * piece, piece)
            held_ref[pl.ds(at, piece), :] = got_ref[m * piece : (m + 1) * piece, :]
    eye = one_hot(iota((width, width), 0) == iota((width, width), 1))
    grad_gate_ref[...] = mm(eye, held_ref[0:hidden, :], 1, 1)
    grad_up_ref[...] = mm(eye, held_ref[hidden : 2 * hidden, :], 1, 1)
    grad_down_ref[...] = held_ref[2 * hidden :, :].astype(F32)


def merge_kernel(cap, table_ref, recv_ref, tok_ref, route_ref):
    top, tok = route_ref.shape
    rows, width = recv_ref.shape
    recv = recv_ref[...]
    slot = iota((rows, tok), 0)
    sub = iota((width, tok), 0)
    first, rank = (table_ref[i * top : (i + 1) * top, :].astype(jnp.int32) for i in range(2))
    hots, scores = [], []
    for j in range(top):
        at, own = first[j : j + 1, :], rank[j : j + 1, :]
        hots.append(jnp.where(slot == at + own, 1.0, 0.0))
        line = mm(recv, one_hot(slot == at + cap), 0, 0)
        scores.append(jnp.sum(jnp.where(sub == own, line, 0.0), axis=0, keepdims=True))
    tok_ref[...] = mm(functools.reduce(jnp.add, hots).astype(BF16), recv, 0, 0).astype(BF16)
    route_ref[...] = jnp.concatenate(scores, axis=0) * table_ref[2 * top : 3 * top, :]


def exchange(rows, axis, groups=None):
    n = lax.axis_size(axis) if groups is None else len(groups[0])
    axis = axis if groups is None else ("exp", "attn")
    blocks = rows.reshape(n, rows.shape[0] // n, rows.shape[1])
    blocks = lax.all_to_all(
        blocks, axis, split_axis=0, concat_axis=0, tiled=True, axis_index_groups=groups
    )
    return blocks.reshape(rows.shape)


def device_groups(experts, parts, local):
    strided, near, far = parts // local, [], []
    for e in range(experts):
        shift = e % 2 * (local // 2)
        place = [
            [
                e * parts + (q * local + (r ^ (local // 2 if 2 * q >= strided else 0)) + shift) % parts
                for r in range(local)
            ]
            for q in range(strided)
        ]
        near += place
        far += [list(column) for column in zip(*place)]
    return near, far


def numbers(parts, local):
    strided = parts // local
    at = (lax.axis_index("attn") + parts - lax.axis_index("exp") % 2 * (local // 2)) % parts
    near = at % local ^ jnp.where(2 * (at // local) >= strided, local // 2, 0)
    return (at // local * 16 + near).reshape(1)


def swap(chunks, groups):
    out = [chunks[0]]
    for k in range(1, len(chunks)):
        pairs = [(group[r], group[r ^ k]) for group in groups for r in range(len(group))]
        out.append(lax.ppermute(chunks[k], ("exp", "attn"), pairs))
    return out


def call(kernel, operands, room=48 * 2**20, **options):
    params = pltpu.CompilerParams(vmem_limit_bytes=VMEM - room)
    specs = [pl.BlockSpec(memory_space=pltpu.SMEM if x.ndim == 1 else pltpu.VMEM) for x in operands]
    return pl.pallas_call(kernel, in_specs=specs, compiler_params=params, **options)(*operands)


def call_fetching(kernel, plain, fetched, scratch=(), **options):
    def body(*refs):
        n, m = len(plain), len(fetched)
        sources, sem = refs[n : n + m], refs[-1]
        held = refs[len(refs) - 1 - m : -1]
        copies = [pltpu.make_async_copy(sources[i], held[i], sem.at[i]) for i in range(m)]
        for copy in copies:
            copy.start()

        def ready():
            for copy in copies:
                copy.wait()

        kernel(ready, *refs[:n], *held, *refs[n + m : len(refs) - 1 - m])

    space = [pltpu.SMEM if x.ndim == 1 else pltpu.VMEM for x in plain] + [pltpu.HBM] * len(fetched)
    return pl.pallas_call(
        body,
        in_specs=[pl.BlockSpec(memory_space=x) for x in space],
        scratch_shapes=list(scratch)
        + [pltpu.VMEM(x.shape, x.dtype) for x in fetched]
        + [pltpu.SemaphoreType.DMA((len(fetched),))],
        compiler_params=pltpu.CompilerParams(vmem_limit_bytes=VMEM),
        **options,
    )(*plain, *fetched)


def shape_of(*dims, dtype=BF16):
    return jax.ShapeDtypeStruct(dims, dtype)


def shards(tokens, cotangent, expert_ids, route_weight, gate_weight, up_weight, down_weight):
    tok, width = tokens.shape
    top = expert_ids.shape[1]
    experts, parts = lax.axis_size("exp"), lax.axis_size("attn")
    cap = 3 * tok * top // (2 * experts)
    hidden = gate_weight.shape[2]
    slots, padded = experts * cap, experts * PAD
    local = math.isqrt(parts)
    strided = parts // local
    piece = hidden // local
    near, far = device_groups(experts, parts, local)
    me = numbers(parts, local)
    ids, weight = expert_ids.T, route_weight.T
    gate_w, up_w, down_w = gate_weight[0], up_weight[0], down_weight[0]

    send, table = call_fetching(
        pack_kernel,
        (),
        (ids, weight, tokens, cotangent),
        out_shape=(shape_of(padded, 2 * width), shape_of(3 * top, tok, dtype=F32)),
        name="pack",
    )
    recv = exchange(send, "exp")
    chunks = call_fetching(
        functools.partial(turn_kernel, local),
        (me,),
        (gate_w, up_w, down_w),
        scratch=[pltpu.VMEM((3 * hidden, width), BF16)],
        out_shape=(shape_of(3 * piece, width),) * local,
        name="turn",
    )
    chunks = swap(chunks, near)
    chunk = piece // strided
    held, scaled = call(
        functools.partial(spread_kernel, cap, local),
        (recv,),
        out_shape=(shape_of(local * slots, width), shape_of(slots, width)),
        name="spread",
    )
    held = exchange(held, "attn", near)
    scaled = swap([scaled] * local, near)
    part = call(
        functools.partial(partial_kernel, slots, strided),
        (me, held, *chunks),
        out_shape=shape_of(2 * piece, slots),
        name="partial",
    )
    part = exchange(part, "attn", far)
    backs = call(
        functools.partial(upstream_kernel, local),
        (me, *scaled, *chunks),
        out_shape=(shape_of(chunk, slots),) * strided,
        scratch_shapes=[pltpu.VMEM((piece, slots), BF16)],
        name="upstream",
    )
    backs = swap(backs, far)
    pair, act = call(
        functools.partial(act_kernel, strided),
        (part, *backs),
        out_shape=(shape_of(2 * piece + strided * PAD, slots), shape_of(chunk, slots)),
        name="acts",
    )
    pair = exchange(pair, "attn", far)
    act = swap([act] * strided, far)
    terms = call(
        functools.partial(term_kernel, strided),
        (me, pair, *chunks),
        out_shape=shape_of(local * (slots + PAD), width),
        name="terms",
    )
    terms = exchange(terms, "attn", near)
    got = call(
        functools.partial(grad_kernel, strided, local),
        (me, held, pair, *act, *scaled),
        out_shape=(shape_of(3 * piece, width),) * local,
        scratch_shapes=[pltpu.VMEM((piece, slots), BF16)],
        name="grads",
    )
    got = swap(got, near)
    back = call(
        functools.partial(back_kernel, cap, slots, local),
        (terms,),
        out_shape=shape_of(padded, width),
        name="back",
    )
    grad_gate, grad_up, grad_down = call(
        out_kernel,
        (me, *got),
        out_shape=(
            shape_of(width, hidden, dtype=F32),
            shape_of(width, hidden, dtype=F32),
            shape_of(hidden, width, dtype=F32),
        ),
        scratch_shapes=[pltpu.VMEM((3 * hidden, width), BF16)],
        name="out",
    )
    grad_tokens, grad_route = call(
        functools.partial(merge_kernel, cap),
        (table, exchange(back, "exp")),
        out_shape=(shape_of(tok, width), shape_of(top, tok, dtype=F32)),
        name="merge",
    )
    return grad_tokens, grad_route.T, grad_gate[None], grad_up[None], grad_down[None]


def solution(mesh):
    in_specs = (
        P("exp", "attn"),
        P("exp", "attn"),
        P("exp", None),
        P("exp", None),
        P("exp", "attn", None),
        P("exp", "attn", None),
        P("exp", None, "attn"),
    )
    out_specs = (
        P("exp", "attn"),
        P("exp", None),
        P("exp", "attn", None),
        P("exp", "attn", None),
        P("exp", None, "attn"),
    )
    return jax.shard_map(shards, mesh=mesh, in_specs=in_specs, out_specs=out_specs, check_vma=False)
```

```python
import functools
import math

import jax
import jax.numpy as jnp
from jax import lax
from jax.experimental import pallas as pl
from jax.experimental.pallas import tpu as pltpu
from jax.sharding import PartitionSpec as P


F32 = jnp.float32
BF16 = jnp.bfloat16
VMEM = 67043328
PAD = 8


def iota(shape, axis):
    return lax.broadcasted_iota(jnp.int32, shape, axis)


def one_hot(mask):
    return jnp.where(mask, 1.0, 0.0).astype(BF16)


def mm(a, b, ca, cb):
    return lax.dot_general(a, b, (((ca,), (cb,)), ((), ())), preferred_element_type=F32)


def pack_kernel(ready, ids_ref, weight_ref, tok_ref, cot_ref, send_ref, table_ref):
    ready()
    top, tok = ids_ref.shape
    rows = send_ref.shape[0]
    width = tok_ref.shape[1]
    ids = ids_ref[...]
    weight = weight_ref[...].astype(F32)
    row, col = iota((tok, tok), 0), iota((tok, tok), 1)
    columns = [
        jnp.sum(jnp.where(row == col, ids[j : j + 1, :], 0), axis=1, keepdims=True)
        for j in range(top)
    ]
    ranks, hots, scaled = [], [], []
    slot = iota((rows, tok), 0)
    for j in range(top):
        same = [jnp.where((columns[i] == ids[j : j + 1, :]) & (row < col), 1, 0) for i in range(top)]
        rank = jnp.sum(functools.reduce(jnp.add, same), axis=0, keepdims=True)
        ranks.append(rank)
        hit = slot == ids[j : j + 1, :] * PAD + rank
        hots.append(jnp.where(hit, 1.0, 0.0))
        scaled.append(jnp.where(hit, weight[j : j + 1, :], 0.0))
    firsts = [ids[j : j + 1, :] * PAD for j in range(top)]
    table = jnp.concatenate(firsts + ranks, axis=0).astype(F32)
    table_ref[...] = jnp.concatenate([table, 1.0 / weight], axis=0)
    plain = functools.reduce(jnp.add, hots).astype(BF16)
    heavy = functools.reduce(jnp.add, scaled).astype(BF16)
    send_ref[:, :width] = mm(plain, tok_ref[...], 1, 0).astype(BF16)
    send_ref[:, width:] = mm(heavy, cot_ref[...], 1, 0).astype(BF16)


def turn_kernel(local, ready, near_ref, gate_ref, up_ref, down_ref, *chunk_refs):
    *chunk_refs, held_ref = chunk_refs
    width, hidden = gate_ref.shape
    piece = hidden // local
    eye = one_hot(iota((width, width), 0) == iota((width, width), 1))
    ready()
    for m, ref in enumerate((gate_ref, up_ref)):
        held_ref[m * hidden : (m + 1) * hidden, :] = mm(ref[...], eye, 0, 0).astype(BF16)
    held_ref[2 * hidden : 3 * hidden, :] = down_ref[...]
    for k, chunk_ref in enumerate(chunk_refs):
        peer = (near_ref[0] & 15) ^ k
        for m in range(3):
            at = pl.multiple_of(m * hidden + peer * piece, piece)
            chunk_ref[m * piece : (m + 1) * piece, :] = held_ref[pl.ds(at, piece), :]


def spread_kernel(cap, local, recv_ref, out_ref, scaled_ref):
    padded = recv_ref.shape[0]
    slots, width = scaled_ref.shape
    s, r = iota((slots, padded), 0), iota((slots, padded), 1)
    keep = one_hot(((r >> 3) * cap + (r & 7) == s) & ((r & 7) < cap))
    rows = mm(keep, recv_ref[...], 1, 0).astype(BF16)
    for p in range(local):
        out_ref[p * slots : (p + 1) * slots, :] = rows[:, :width]
    scaled_ref[...] = rows[:, width:]


def rows_of(held_ref, me_ref, k, slots):
    return held_ref[pl.ds(pl.multiple_of(((me_ref[0] & 15) ^ k) * slots, 16), slots), :]


def partial_kernel(slots, strided, me_ref, held_ref, *refs):
    *weight_refs, part_ref = refs
    piece = weight_refs[0].shape[0] // 3
    chunk = piece // strided
    for m in range(2):
        total = None
        for k, weight_ref in enumerate(weight_refs):
            rows = rows_of(held_ref, me_ref, k, slots)
            term = mm(weight_ref[m * piece : (m + 1) * piece, :], rows, 1, 1)
            total = term if total is None else total + term
        total = total.astype(BF16)
        for q in range(strided):
            to = (q * 2 + m) * chunk
            part_ref[to : to + chunk, :] = total[q * chunk : (q + 1) * chunk, :]


def upstream_kernel(n, me_ref, *refs):
    scaled_refs, weight_refs, chunk_refs, held_ref = refs[:n], refs[n : 2 * n], refs[2 * n : -1], refs[-1]
    piece = weight_refs[0].shape[0] // 3
    chunk = chunk_refs[0].shape[0]
    total = None
    for scaled_ref, weight_ref in zip(scaled_refs, weight_refs):
        term = mm(weight_ref[2 * piece :, :], scaled_ref[...], 1, 1)
        total = term if total is None else total + term
    held_ref[...] = total.astype(BF16)
    for k, chunk_ref in enumerate(chunk_refs):
        at = pl.multiple_of(((me_ref[0] >> 4) ^ k) * chunk, 16)
        chunk_ref[...] = held_ref[pl.ds(at, chunk), :]


def act_kernel(strided, part_ref, *refs):
    *back_refs, out_ref = refs
    n = part_ref.shape[0] // strided
    chunk = n // 2
    total = part_ref[0:n, :].astype(F32)
    for q in range(1, strided):
        total = total + part_ref[q * n : (q + 1) * n, :].astype(F32)
    gate, up = total[:chunk, :], total[chunk:, :]
    back = functools.reduce(jnp.add, [ref[...].astype(F32) for ref in back_refs])
    sig = jax.nn.sigmoid(gate)
    silu = gate * sig
    act = (silu * up).astype(BF16)
    grad_g = (back * up * sig * (1.0 + gate * (1.0 - sig))).astype(BF16)
    grad_u = (back * silu).astype(BF16)
    score = jnp.sum(act.astype(F32) * back, axis=0, keepdims=True)
    score = jnp.where(iota((PAD, score.shape[1]), 0) == 0, score, 0.0).astype(BF16)
    m = out_ref.shape[0] // strided
    for q in range(strided):
        at = q * m
        out_ref[at : at + chunk, :] = grad_g
        out_ref[at + chunk : at + n, :] = grad_u
        out_ref[at + n : at + n + chunk, :] = act
        out_ref[at + n + chunk : at + m, :] = score


def three_of(acts_ref, strided):
    m = acts_ref.shape[0] // strided
    chunk = (m - PAD) // 3
    return [
        jnp.concatenate(
            [acts_ref[q * m + k * chunk : q * m + (k + 1) * chunk, :] for q in range(strided)], axis=0
        )
        for k in range(3)
    ]


def term_kernel(strided, me_ref, acts_ref, *refs):
    *weight_refs, out_ref = refs
    slots = acts_ref.shape[1]
    width = out_ref.shape[1]
    piece = weight_refs[0].shape[0] // 3
    m = acts_ref.shape[0] // strided
    grad_g, grad_u, _ = three_of(acts_ref, strided)
    score = acts_ref[m - PAD : m, :].astype(F32)
    for q in range(1, strided):
        score = score + acts_ref[(q + 1) * m - PAD : (q + 1) * m, :].astype(F32)
    lines = slots // width
    score = jnp.concatenate(
        [score[0:1, k * width : (k + 1) * width] for k in range(lines)]
        + [jnp.zeros((PAD - lines, width), F32)],
        axis=0,
    ).astype(BF16)
    for k, weight_ref in enumerate(weight_refs):
        gate_w, up_w = weight_ref[0:piece, :], weight_ref[piece : 2 * piece, :]
        to = pl.multiple_of(((me_ref[0] & 15) ^ k) * (slots + PAD), PAD)
        out_ref[pl.ds(to, slots), :] = (mm(grad_g, gate_w, 0, 0) + mm(grad_u, up_w, 0, 0)).astype(BF16)
        out_ref[pl.ds(to + slots, PAD), :] = score


def grad_kernel(strided, local, me_ref, held_ref, acts_ref, *refs):
    scaled_refs, out_refs = refs[:local], refs[local:]
    slots = acts_ref.shape[1]
    piece = out_refs[0].shape[0] // 3
    grad_g, grad_u, act = three_of(acts_ref, strided)
    for k, out_ref in enumerate(out_refs):
        feat = rows_of(held_ref, me_ref, k, slots)
        out_ref[0:piece, :] = mm(grad_g, feat, 1, 0).astype(BF16)
        out_ref[piece : 2 * piece, :] = mm(grad_u, feat, 1, 0).astype(BF16)
        out_ref[2 * piece : 3 * piece, :] = mm(act, scaled_refs[k][...], 1, 0).astype(BF16)


def back_kernel(cap, slots, local, got_ref, send_ref):
    padded, width = send_ref.shape
    block = got_ref.shape[0] // local
    term = got_ref[0 : slots + PAD, :].astype(F32)
    for f in range(1, local):
        term = term + got_ref[f * block : f * block + slots + PAD, :].astype(F32)
    lines = slots // width
    score = jnp.concatenate([term[slots + k : slots + k + 1, :] for k in range(lines)], axis=1)
    term = term[:slots, :].astype(BF16)
    r, s = iota((padded, slots), 0), iota((padded, slots), 1)
    spread = one_hot(((r >> 3) * cap + (r & 7) == s) & ((r & 7) < cap))
    base = (r >> 3) * cap
    mine = ((r & 7) == cap) & (s >= base) & (s < base + cap)
    scores = jnp.where(mine, score, 0.0).astype(BF16)
    lane = one_hot(lax.rem(iota((slots, width), 0), cap) == iota((slots, width), 1))
    send_ref[...] = (mm(spread, term, 1, 0) + mm(scores, lane, 1, 0)).astype(BF16)


def out_kernel(near_ref, *refs):
    *got_refs, grad_gate_ref, grad_up_ref, grad_down_ref, held_ref = refs
    piece, width = got_refs[0].shape[0] // 3, got_refs[0].shape[1]
    hidden = piece * len(got_refs)
    for k, got_ref in enumerate(got_refs):
        for m in range(3):
            at = pl.multiple_of(m * hidden + ((near_ref[0] & 15) ^ k) * piece, piece)
            held_ref[pl.ds(at, piece), :] = got_ref[m * piece : (m + 1) * piece, :]
    eye = one_hot(iota((width, width), 0) == iota((width, width), 1))
    grad_gate_ref[...] = mm(eye, held_ref[0:hidden, :], 1, 1)
    grad_up_ref[...] = mm(eye, held_ref[hidden : 2 * hidden, :], 1, 1)
    grad_down_ref[...] = held_ref[2 * hidden :, :].astype(F32)


def merge_kernel(cap, table_ref, recv_ref, tok_ref, route_ref):
    top, tok = route_ref.shape
    rows, width = recv_ref.shape
    recv = recv_ref[...]
    slot = iota((rows, tok), 0)
    sub = iota((width, tok), 0)
    first, rank = (table_ref[i * top : (i + 1) * top, :].astype(jnp.int32) for i in range(2))
    hots, scores = [], []
    for j in range(top):
        at, own = first[j : j + 1, :], rank[j : j + 1, :]
        hots.append(jnp.where(slot == at + own, 1.0, 0.0))
        line = mm(recv, one_hot(slot == at + cap), 0, 0)
        scores.append(jnp.sum(jnp.where(sub == own, line, 0.0), axis=0, keepdims=True))
    tok_ref[...] = mm(functools.reduce(jnp.add, hots).astype(BF16), recv, 0, 0).astype(BF16)
    route_ref[...] = jnp.concatenate(scores, axis=0) * table_ref[2 * top : 3 * top, :]


def exchange(rows, axis, groups=None):
    n = lax.axis_size(axis) if groups is None else len(groups[0])
    axis = axis if groups is None else ("exp", "attn")
    blocks = rows.reshape(n, rows.shape[0] // n, rows.shape[1])
    blocks = lax.all_to_all(
        blocks, axis, split_axis=0, concat_axis=0, tiled=True, axis_index_groups=groups
    )
    return blocks.reshape(rows.shape)


def device_groups(experts, parts, local):
    strided, near, far = parts // local, [], []
    for e in range(experts):
        shift = e % 2 * (local // 2)
        place = [
            [
                e * parts + (q * local + (r ^ (local // 2 if 2 * q >= strided else 0)) + shift) % parts
                for r in range(local)
            ]
            for q in range(strided)
        ]
        near += place
        far += [list(column) for column in zip(*place)]
    return near, far


def numbers(parts, local):
    strided = parts // local
    at = (lax.axis_index("attn") + parts - lax.axis_index("exp") % 2 * (local // 2)) % parts
    near = at % local ^ jnp.where(2 * (at // local) >= strided, local // 2, 0)
    return (at // local * 16 + near).reshape(1)


def swap(chunks, groups):
    out = [chunks[0]]
    for k in range(1, len(chunks)):
        pairs = [(group[r], group[r ^ k]) for group in groups for r in range(len(group))]
        out.append(lax.ppermute(chunks[k], ("exp", "attn"), pairs))
    return out


def call(kernel, operands, room=48 * 2**20, **options):
    params = pltpu.CompilerParams(vmem_limit_bytes=VMEM - room)
    specs = [pl.BlockSpec(memory_space=pltpu.SMEM if x.ndim == 1 else pltpu.VMEM) for x in operands]
    return pl.pallas_call(kernel, in_specs=specs, compiler_params=params, **options)(*operands)


def call_fetching(kernel, plain, fetched, scratch=(), **options):
    def body(*refs):
        n, m = len(plain), len(fetched)
        sources, sem = refs[n : n + m], refs[-1]
        held = refs[len(refs) - 1 - m : -1]
        copies = [pltpu.make_async_copy(sources[i], held[i], sem.at[i]) for i in range(m)]
        for copy in copies:
            copy.start()

        def ready():
            for copy in copies:
                copy.wait()

        kernel(ready, *refs[:n], *held, *refs[n + m : len(refs) - 1 - m])

    space = [pltpu.SMEM if x.ndim == 1 else pltpu.VMEM for x in plain] + [pltpu.HBM] * len(fetched)
    return pl.pallas_call(
        body,
        in_specs=[pl.BlockSpec(memory_space=x) for x in space],
        scratch_shapes=list(scratch)
        + [pltpu.VMEM(x.shape, x.dtype) for x in fetched]
        + [pltpu.SemaphoreType.DMA((len(fetched),))],
        compiler_params=pltpu.CompilerParams(vmem_limit_bytes=VMEM),
        **options,
    )(*plain, *fetched)


def shape_of(*dims, dtype=BF16):
    return jax.ShapeDtypeStruct(dims, dtype)


def shards(tokens, cotangent, expert_ids, route_weight, gate_weight, up_weight, down_weight):
    tok, width = tokens.shape
    top = expert_ids.shape[1]
    experts, parts = lax.axis_size("exp"), lax.axis_size("attn")
    cap = 3 * tok * top // (2 * experts)
    hidden = gate_weight.shape[2]
    slots, padded = experts * cap, experts * PAD
    local = math.isqrt(parts)
    strided = parts // local
    piece = hidden // local
    near, far = device_groups(experts, parts, local)
    me = numbers(parts, local)
    ids, weight = expert_ids.T, route_weight.T
    gate_w, up_w, down_w = gate_weight[0], up_weight[0], down_weight[0]

    send, table = call_fetching(
        pack_kernel,
        (),
        (ids, weight, tokens, cotangent),
        out_shape=(shape_of(padded, 2 * width), shape_of(3 * top, tok, dtype=F32)),
        name="pack",
    )
    recv = exchange(send, "exp")
    chunks = call_fetching(
        functools.partial(turn_kernel, local),
        (me,),
        (gate_w, up_w, down_w),
        scratch=[pltpu.VMEM((3 * hidden, width), BF16)],
        out_shape=(shape_of(3 * piece, width),) * local,
        name="turn",
    )
    chunks = swap(chunks, near)
    chunk = piece // strided
    held, scaled = call(
        functools.partial(spread_kernel, cap, local),
        (recv,),
        out_shape=(shape_of(local * slots, width), shape_of(slots, width)),
        name="spread",
    )
    held = exchange(held, "attn", near)
    scaled = swap([scaled] * local, near)
    part = call(
        functools.partial(partial_kernel, slots, strided),
        (me, held, *chunks),
        out_shape=shape_of(2 * piece, slots),
        name="partial",
    )
    part = exchange(part, "attn", far)
    backs = call(
        functools.partial(upstream_kernel, local),
        (me, *scaled, *chunks),
        out_shape=(shape_of(chunk, slots),) * strided,
        scratch_shapes=[pltpu.VMEM((piece, slots), BF16)],
        name="upstream",
    )
    backs = swap(backs, far)
    acts = call(
        functools.partial(act_kernel, strided),
        (part, *backs),
        out_shape=shape_of(3 * piece + strided * PAD, slots),
        name="acts",
    )
    acts = exchange(acts, "attn", far)
    terms = call(
        functools.partial(term_kernel, strided),
        (me, acts, *chunks),
        out_shape=shape_of(local * (slots + PAD), width),
        name="terms",
    )
    terms = exchange(terms, "attn", near)
    got = call(
        functools.partial(grad_kernel, strided, local),
        (me, held, acts, *scaled),
        out_shape=(shape_of(3 * piece, width),) * local,
        name="grads",
    )
    got = swap(got, near)
    back = call(
        functools.partial(back_kernel, cap, slots, local),
        (terms,),
        out_shape=shape_of(padded, width),
        name="back",
    )
    grad_gate, grad_up, grad_down = call(
        out_kernel,
        (me, *got),
        out_shape=(
            shape_of(width, hidden, dtype=F32),
            shape_of(width, hidden, dtype=F32),
            shape_of(hidden, width, dtype=F32),
        ),
        scratch_shapes=[pltpu.VMEM((3 * hidden, width), BF16)],
        name="out",
    )
    grad_tokens, grad_route = call(
        functools.partial(merge_kernel, cap),
        (table, exchange(back, "exp")),
        out_shape=(shape_of(tok, width), shape_of(top, tok, dtype=F32)),
        name="merge",
    )
    return grad_tokens, grad_route.T, grad_gate[None], grad_up[None], grad_down[None]


def solution(mesh):
    in_specs = (
        P("exp", "attn"),
        P("exp", "attn"),
        P("exp", None),
        P("exp", None),
        P("exp", "attn", None),
        P("exp", "attn", None),
        P("exp", None, "attn"),
    )
    out_specs = (
        P("exp", "attn"),
        P("exp", None),
        P("exp", "attn", None),
        P("exp", "attn", None),
        P("exp", None, "attn"),
    )
    return jax.shard_map(shards, mesh=mesh, in_specs=in_specs, out_specs=out_specs, check_vma=False)
```

```python
import functools
import math

import jax
import jax.numpy as jnp
from jax import lax
from jax.experimental import pallas as pl
from jax.experimental.pallas import tpu as pltpu
from jax.sharding import PartitionSpec as P


F32 = jnp.float32
BF16 = jnp.bfloat16
VMEM = 67043328
PAD = 8


def iota(shape, axis):
    return lax.broadcasted_iota(jnp.int32, shape, axis)


def one_hot(mask):
    return jnp.where(mask, 1.0, 0.0).astype(BF16)


def mm(a, b, ca, cb):
    return lax.dot_general(a, b, (((ca,), (cb,)), ((), ())), preferred_element_type=F32)


def pack_kernel(ready, ids_ref, weight_ref, tok_ref, cot_ref, send_ref, table_ref):
    ready()
    top, tok = ids_ref.shape
    rows = send_ref.shape[0]
    width = tok_ref.shape[1]
    ids = ids_ref[...]
    weight = weight_ref[...].astype(F32)
    row, col = iota((tok, tok), 0), iota((tok, tok), 1)
    columns = [
        jnp.sum(jnp.where(row == col, ids[j : j + 1, :], 0), axis=1, keepdims=True)
        for j in range(top)
    ]
    ranks, hots, scaled = [], [], []
    slot = iota((rows, tok), 0)
    for j in range(top):
        same = [jnp.where((columns[i] == ids[j : j + 1, :]) & (row < col), 1, 0) for i in range(top)]
        rank = jnp.sum(functools.reduce(jnp.add, same), axis=0, keepdims=True)
        ranks.append(rank)
        hit = slot == ids[j : j + 1, :] * PAD + rank
        hots.append(jnp.where(hit, 1.0, 0.0))
        scaled.append(jnp.where(hit, weight[j : j + 1, :], 0.0))
    firsts = [ids[j : j + 1, :] * PAD for j in range(top)]
    table = jnp.concatenate(firsts + ranks, axis=0).astype(F32)
    table_ref[...] = jnp.concatenate([table, 1.0 / weight], axis=0)
    plain = functools.reduce(jnp.add, hots).astype(BF16)
    heavy = functools.reduce(jnp.add, scaled).astype(BF16)
    send_ref[:, :width] = mm(plain, tok_ref[...], 1, 0).astype(BF16)
    send_ref[:, width:] = mm(heavy, cot_ref[...], 1, 0).astype(BF16)


def turn_kernel(local, ready, near_ref, gate_ref, up_ref, down_ref, *chunk_refs):
    *chunk_refs, held_ref = chunk_refs
    width, hidden = gate_ref.shape
    piece = hidden // local
    eye = one_hot(iota((width, width), 0) == iota((width, width), 1))
    ready()
    for m, ref in enumerate((gate_ref, up_ref)):
        held_ref[m * hidden : (m + 1) * hidden, :] = mm(ref[...], eye, 0, 0).astype(BF16)
    held_ref[2 * hidden : 3 * hidden, :] = down_ref[...]
    for k, chunk_ref in enumerate(chunk_refs):
        peer = (near_ref[0] & 15) ^ k
        for m in range(3):
            at = pl.multiple_of(m * hidden + peer * piece, piece)
            chunk_ref[m * piece : (m + 1) * piece, :] = held_ref[pl.ds(at, piece), :]


def spread_kernel(cap, local, recv_ref, out_ref):
    padded = recv_ref.shape[0]
    width = out_ref.shape[1]
    slots = padded // PAD * cap
    s, r = iota((slots, padded), 0), iota((slots, padded), 1)
    keep = one_hot(((r >> 3) * cap + (r & 7) == s) & ((r & 7) < cap))
    rows = mm(keep, recv_ref[...], 1, 0).astype(BF16)
    for p in range(local):
        at = p * 2 * slots
        out_ref[at : at + slots, :] = rows[:, :width]
        out_ref[at + slots : at + 2 * slots, :] = rows[:, width:]


def rows_of(held_ref, near_ref, k, slots, scaled):
    at = pl.multiple_of(((near_ref[0] & 15) ^ k) * (2 * slots) + slots * scaled, 16)
    return held_ref[pl.ds(at, slots), :]


def partial_kernel(slots, strided, near_ref, held_ref, *refs):
    *weight_refs, part_ref = refs
    piece = weight_refs[0].shape[0] // 3
    chunk = piece // strided
    for m in range(3):
        total = None
        for k, weight_ref in enumerate(weight_refs):
            rows = rows_of(held_ref, near_ref, k, slots, m // 2)
            term = mm(weight_ref[m * piece : (m + 1) * piece, :], rows, 1, 1)
            total = term if total is None else total + term
        total = total.astype(BF16)
        for q in range(strided):
            to = (q * 3 + m) * chunk
            part_ref[to : to + chunk, :] = total[q * chunk : (q + 1) * chunk, :]


def act_kernel(strided, part_ref, out_ref, act_ref):
    n = part_ref.shape[0] // strided
    chunk = n // 3
    total = part_ref[0:n, :].astype(F32)
    for q in range(1, strided):
        total = total + part_ref[q * n : (q + 1) * n, :].astype(F32)
    gate, up, back = (total[m * chunk : (m + 1) * chunk, :] for m in range(3))
    sig = jax.nn.sigmoid(gate)
    silu = gate * sig
    act = (silu * up).astype(BF16)
    grad_g = (back * up * sig * (1.0 + gate * (1.0 - sig))).astype(BF16)
    grad_u = (back * silu).astype(BF16)
    score = jnp.sum(act.astype(F32) * back, axis=0, keepdims=True)
    score = jnp.where(iota((PAD, score.shape[1]), 0) == 0, score, 0.0).astype(BF16)
    act_ref[...] = act
    m = out_ref.shape[0] // strided
    for q in range(strided):
        at = q * m
        out_ref[at : at + chunk, :] = grad_g
        out_ref[at + chunk : at + 2 * chunk, :] = grad_u
        out_ref[at + 2 * chunk : at + m, :] = score


def pair_of(pair_ref, strided):
    m = pair_ref.shape[0] // strided
    chunk = (m - PAD) // 2
    return [
        jnp.concatenate(
            [pair_ref[q * m + k * chunk : q * m + (k + 1) * chunk, :] for q in range(strided)], axis=0
        )
        for k in range(2)
    ]


def term_kernel(strided, me_ref, pair_ref, *refs):
    *weight_refs, out_ref = refs
    slots = pair_ref.shape[1]
    width = out_ref.shape[1]
    piece = weight_refs[0].shape[0] // 3
    m = pair_ref.shape[0] // strided
    grad_g, grad_u = pair_of(pair_ref, strided)
    score = pair_ref[m - PAD : m, :].astype(F32)
    for q in range(1, strided):
        score = score + pair_ref[(q + 1) * m - PAD : (q + 1) * m, :].astype(F32)
    lines = slots // width
    score = jnp.concatenate(
        [score[0:1, k * width : (k + 1) * width] for k in range(lines)]
        + [jnp.zeros((PAD - lines, width), F32)],
        axis=0,
    ).astype(BF16)
    for k, weight_ref in enumerate(weight_refs):
        gate_w, up_w = weight_ref[0:piece, :], weight_ref[piece : 2 * piece, :]
        to = pl.multiple_of(((me_ref[0] & 15) ^ k) * (slots + PAD), PAD)
        out_ref[pl.ds(to, slots), :] = (mm(grad_g, gate_w, 0, 0) + mm(grad_u, up_w, 0, 0)).astype(BF16)
        out_ref[pl.ds(to + slots, PAD), :] = score


def grad_kernel(strided, me_ref, held_ref, pair_ref, *refs):
    act_refs, out_refs, act_ref = refs[:strided], refs[strided:-1], refs[-1]
    slots = pair_ref.shape[1]
    piece = out_refs[0].shape[0] // 3
    chunk = piece // strided
    grad_g, grad_u = pair_of(pair_ref, strided)
    for k, ref in enumerate(act_refs):
        act_ref[pl.ds(pl.multiple_of(((me_ref[0] >> 4) ^ k) * chunk, 16), chunk), :] = ref[...]
    for k, out_ref in enumerate(out_refs):
        feat = rows_of(held_ref, me_ref, k, slots, 0)
        scaled = rows_of(held_ref, me_ref, k, slots, 1)
        out_ref[0:piece, :] = mm(grad_g, feat, 1, 0).astype(BF16)
        out_ref[piece : 2 * piece, :] = mm(grad_u, feat, 1, 0).astype(BF16)
        out_ref[2 * piece : 3 * piece, :] = mm(act_ref[...], scaled, 1, 0).astype(BF16)


def back_kernel(cap, slots, local, got_ref, send_ref):
    padded, width = send_ref.shape
    block = got_ref.shape[0] // local
    term = got_ref[0 : slots + PAD, :].astype(F32)
    for f in range(1, local):
        term = term + got_ref[f * block : f * block + slots + PAD, :].astype(F32)
    lines = slots // width
    score = jnp.concatenate([term[slots + k : slots + k + 1, :] for k in range(lines)], axis=1)
    term = term[:slots, :].astype(BF16)
    r, s = iota((padded, slots), 0), iota((padded, slots), 1)
    spread = one_hot(((r >> 3) * cap + (r & 7) == s) & ((r & 7) < cap))
    base = (r >> 3) * cap
    mine = ((r & 7) == cap) & (s >= base) & (s < base + cap)
    scores = jnp.where(mine, score, 0.0).astype(BF16)
    lane = one_hot(lax.rem(iota((slots, width), 0), cap) == iota((slots, width), 1))
    send_ref[...] = (mm(spread, term, 1, 0) + mm(scores, lane, 1, 0)).astype(BF16)


def out_kernel(near_ref, *refs):
    *got_refs, grad_gate_ref, grad_up_ref, grad_down_ref, held_ref = refs
    piece, width = got_refs[0].shape[0] // 3, got_refs[0].shape[1]
    hidden = piece * len(got_refs)
    for k, got_ref in enumerate(got_refs):
        for m in range(3):
            at = pl.multiple_of(m * hidden + ((near_ref[0] & 15) ^ k) * piece, piece)
            held_ref[pl.ds(at, piece), :] = got_ref[m * piece : (m + 1) * piece, :]
    eye = one_hot(iota((width, width), 0) == iota((width, width), 1))
    grad_gate_ref[...] = mm(eye, held_ref[0:hidden, :], 1, 1)
    grad_up_ref[...] = mm(eye, held_ref[hidden : 2 * hidden, :], 1, 1)
    grad_down_ref[...] = held_ref[2 * hidden :, :].astype(F32)


def merge_kernel(cap, table_ref, recv_ref, tok_ref, route_ref):
    top, tok = route_ref.shape
    rows, width = recv_ref.shape
    recv = recv_ref[...]
    slot = iota((rows, tok), 0)
    sub = iota((width, tok), 0)
    first, rank = (table_ref[i * top : (i + 1) * top, :].astype(jnp.int32) for i in range(2))
    hots, scores = [], []
    for j in range(top):
        at, own = first[j : j + 1, :], rank[j : j + 1, :]
        hots.append(jnp.where(slot == at + own, 1.0, 0.0))
        line = mm(recv, one_hot(slot == at + cap), 0, 0)
        scores.append(jnp.sum(jnp.where(sub == own, line, 0.0), axis=0, keepdims=True))
    tok_ref[...] = mm(functools.reduce(jnp.add, hots).astype(BF16), recv, 0, 0).astype(BF16)
    route_ref[...] = jnp.concatenate(scores, axis=0) * table_ref[2 * top : 3 * top, :]


def exchange(rows, axis, groups=None):
    n = lax.axis_size(axis) if groups is None else len(groups[0])
    axis = axis if groups is None else ("exp", "attn")
    blocks = rows.reshape(n, rows.shape[0] // n, rows.shape[1])
    blocks = lax.all_to_all(
        blocks, axis, split_axis=0, concat_axis=0, tiled=True, axis_index_groups=groups
    )
    return blocks.reshape(rows.shape)


def device_groups(experts, parts, local):
    strided, near, far = parts // local, [], []
    for e in range(experts):
        shift = e % 2 * (local // 2)
        place = [
            [
                e * parts + (q * local + (r ^ (local // 2 if 2 * q >= strided else 0)) + shift) % parts
                for r in range(local)
            ]
            for q in range(strided)
        ]
        near += place
        far += [list(column) for column in zip(*place)]
    return near, far


def numbers(parts, local):
    strided = parts // local
    at = (lax.axis_index("attn") + parts - lax.axis_index("exp") % 2 * (local // 2)) % parts
    near = at % local ^ jnp.where(2 * (at // local) >= strided, local // 2, 0)
    return (at // local * 16 + near).reshape(1)


def swap(chunks, groups):
    out = [chunks[0]]
    for k in range(1, len(chunks)):
        pairs = [(group[r], group[r ^ k]) for group in groups for r in range(len(group))]
        out.append(lax.ppermute(chunks[k], ("exp", "attn"), pairs))
    return out


def call(kernel, operands, room=48 * 2**20, **options):
    params = pltpu.CompilerParams(vmem_limit_bytes=VMEM - room)
    specs = [pl.BlockSpec(memory_space=pltpu.SMEM if x.ndim == 1 else pltpu.VMEM) for x in operands]
    return pl.pallas_call(kernel, in_specs=specs, compiler_params=params, **options)(*operands)


def call_fetching(kernel, plain, fetched, scratch=(), **options):
    def body(*refs):
        n, m = len(plain), len(fetched)
        sources, sem = refs[n : n + m], refs[-1]
        held = refs[len(refs) - 1 - m : -1]
        copies = [pltpu.make_async_copy(sources[i], held[i], sem.at[i]) for i in range(m)]
        for copy in copies:
            copy.start()

        def ready():
            for copy in copies:
                copy.wait()

        kernel(ready, *refs[:n], *held, *refs[n + m : len(refs) - 1 - m])

    space = [pltpu.SMEM if x.ndim == 1 else pltpu.VMEM for x in plain] + [pltpu.HBM] * len(fetched)
    return pl.pallas_call(
        body,
        in_specs=[pl.BlockSpec(memory_space=x) for x in space],
        scratch_shapes=list(scratch)
        + [pltpu.VMEM(x.shape, x.dtype) for x in fetched]
        + [pltpu.SemaphoreType.DMA((len(fetched),))],
        compiler_params=pltpu.CompilerParams(vmem_limit_bytes=VMEM),
        **options,
    )(*plain, *fetched)


def shape_of(*dims, dtype=BF16):
    return jax.ShapeDtypeStruct(dims, dtype)


def shards(tokens, cotangent, expert_ids, route_weight, gate_weight, up_weight, down_weight):
    tok, width = tokens.shape
    top = expert_ids.shape[1]
    experts, parts = lax.axis_size("exp"), lax.axis_size("attn")
    cap = 3 * tok * top // (2 * experts)
    hidden = gate_weight.shape[2]
    slots, padded = experts * cap, experts * PAD
    local = math.isqrt(parts)
    strided = parts // local
    piece = hidden // local
    near, far = device_groups(experts, parts, local)
    me = numbers(parts, local)
    ids, weight = expert_ids.T, route_weight.T
    gate_w, up_w, down_w = gate_weight[0], up_weight[0], down_weight[0]

    send, table = call_fetching(
        pack_kernel,
        (),
        (ids, weight, tokens, cotangent),
        out_shape=(shape_of(padded, 2 * width), shape_of(3 * top, tok, dtype=F32)),
        name="pack",
    )
    recv = exchange(send, "exp")
    chunks = call_fetching(
        functools.partial(turn_kernel, local),
        (me,),
        (gate_w, up_w, down_w),
        scratch=[pltpu.VMEM((3 * hidden, width), BF16)],
        out_shape=(shape_of(3 * piece, width),) * local,
        name="turn",
    )
    chunks = swap(chunks, near)
    chunk = piece // strided
    held = call(
        functools.partial(spread_kernel, cap, local),
        (recv,),
        out_shape=shape_of(local * 2 * slots, width),
        name="spread",
    )
    held = exchange(held, "attn", near)
    part = call(
        functools.partial(partial_kernel, slots, strided),
        (me, held, *chunks),
        out_shape=shape_of(3 * piece, slots),
        name="partial",
    )
    part = exchange(part, "attn", far)
    pair, act = call(
        functools.partial(act_kernel, strided),
        (part,),
        out_shape=(shape_of(2 * piece + strided * PAD, slots), shape_of(chunk, slots)),
        name="acts",
    )
    pair = exchange(pair, "attn", far)
    act = swap([act] * strided, far)
    terms = call(
        functools.partial(term_kernel, strided),
        (me, pair, *chunks),
        out_shape=shape_of(local * (slots + PAD), width),
        name="terms",
    )
    terms = exchange(terms, "attn", near)
    got = call(
        functools.partial(grad_kernel, strided),
        (me, held, pair, *act),
        out_shape=(shape_of(3 * piece, width),) * local,
        scratch_shapes=[pltpu.VMEM((piece, slots), BF16)],
        name="grads",
    )
    got = swap(got, near)
    back = call(
        functools.partial(back_kernel, cap, slots, local),
        (terms,),
        out_shape=shape_of(padded, width),
        name="back",
    )
    grad_gate, grad_up, grad_down = call(
        out_kernel,
        (me, *got),
        out_shape=(
            shape_of(width, hidden, dtype=F32),
            shape_of(width, hidden, dtype=F32),
            shape_of(hidden, width, dtype=F32),
        ),
        scratch_shapes=[pltpu.VMEM((3 * hidden, width), BF16)],
        name="out",
    )
    grad_tokens, grad_route = call(
        functools.partial(merge_kernel, cap),
        (table, exchange(back, "exp")),
        out_shape=(shape_of(tok, width), shape_of(top, tok, dtype=F32)),
        name="merge",
    )
    return grad_tokens, grad_route.T, grad_gate[None], grad_up[None], grad_down[None]


def solution(mesh):
    in_specs = (
        P("exp", "attn"),
        P("exp", "attn"),
        P("exp", None),
        P("exp", None),
        P("exp", "attn", None),
        P("exp", "attn", None),
        P("exp", None, "attn"),
    )
    out_specs = (
        P("exp", "attn"),
        P("exp", None),
        P("exp", "attn", None),
        P("exp", "attn", None),
        P("exp", None, "attn"),
    )
    return jax.shard_map(shards, mesh=mesh, in_specs=in_specs, out_specs=out_specs, check_vma=False)
```
